32 devices in a mesh: space: 8 (over z, y), chan: 2 (over core), filt: 2 (over x).
Axes of the slice: x: 2, y: 2, z: 4, core: 2. Of those that a mesh axis runs over, the one named last changes fastest.
Arguments:
- activation: bfloat16 [8, 512, 512], P('space', ('chan', 'filt')), may hold values from -6 to 6
- kernel: bfloat16 [3, 3, 3, 512, 512], P(None, None, None, 'filt', 'chan'), may hold values from -0.0546875 to 0.0546875
- out_grad: bfloat16 [8, 512, 512], P('space', 'filt', 'chan'), may hold values from -6 to 6
Outputs:
- output: bfloat16 [8, 512, 512], P('space', 'filt', 'chan')
- input_grad: bfloat16 [8, 512, 512], P('space', ('chan', 'filt'))
- kernel_grad: float32 [3, 3, 3, 512, 512], P(None, None, None, 'filt', 'chan')
The draws below stay inside these ranges and needn't reach their ends.
All inputs are finite; a program needn't handle non-finite values.
Results may differ from the reference program's by a relative error of at most 0.001.
Values may be sent and summed in bfloat16 or wider, within the bound.
A program may use at most 128 MiB of HBM per device.

```python
import jax
import jax.numpy as jnp
from jax import lax

C = 512
F = 512
H = 32
W = 16
NZ = 8


def shard_levels(own_key, shape, split, least, high):
    loudness = 1.0
    for dim, parts in split:
        draws = jax.random.uniform(jax.random.fold_in(jax.random.fold_in(own_key, 6), dim), (parts,), jnp.float32, least / len(split), high / len(split))
        loudness = loudness * jnp.repeat(jnp.exp(draws), shape[dim] // parts).reshape((-1,) + (1,) * (len(shape) - 1 - dim))
    return loudness


def centred(own_key, dims, deviation, bound, cuts=(), kind=jnp.bfloat16):
    level = shard_levels(own_key, dims, cuts, -0.22, 0.18) if cuts else 1.0
    values = jax.random.normal(own_key, dims, jnp.float32) * deviation * level
    return jnp.minimum(jnp.maximum(values, -bound), bound).astype(kind)


def setup_inputs(seed: int = 0) -> dict:
    streams_of = jax.random.split(jax.random.key(seed), 4)
    return {
        "activation": centred(streams_of[0], (NZ, C, H * W), 1.0, 6.0, ((0, 8), (1, 4))),
        "kernel": centred(streams_of[1], (3, 3, 3, F, C), (27 * C) ** -0.5, 0.0546875, ((3, 2), (4, 2))),
        "out_grad": centred(streams_of[2], (NZ, F, H * W), 1.0, 6.0, ((0, 8), (1, 2), (2, 2))),
    }


def reference(activation, kernel, out_grad):
    volume = activation.reshape(NZ, C, H, W).transpose(1, 0, 2, 3)[None]
    result = lax.conv_general_dilated(volume, kernel, (1, 1, 1), 'SAME', dimension_numbers=('NCDHW', 'DHWOI', 'NCDHW'), preferred_element_type=jnp.float32)[0]
    output = result.transpose(1, 0, 2, 3).reshape(NZ, F, H * W).astype(jnp.bfloat16)
    grad_volume = out_grad.reshape(NZ, F, H, W).transpose(1, 0, 2, 3)[None]
    flipped = kernel[::-1, ::-1, ::-1]
    back = lax.conv_general_dilated(grad_volume, flipped, (1, 1, 1), 'SAME', dimension_numbers=('NCDHW', 'DHWIO', 'NCDHW'), preferred_element_type=jnp.float32)[0]
    input_grad = back.transpose(1, 0, 2, 3).reshape(NZ, C, H * W).astype(jnp.bfloat16)
    padded = jnp.pad(activation.reshape(NZ, C, H, W), ((1, 1), (0, 0), (1, 1), (1, 1))).astype(jnp.float32)
    grad_wide = out_grad.astype(jnp.float32)
    taps = []
    for a in range(3):
        for b in range(3):
            for c in range(3):
                piece = padded[a:a + NZ, :, b:b + H, c:c + W].reshape(NZ, C, H * W)
                taps.append(jnp.einsum('zfp,zkp->fk', grad_wide, piece))
    kernel_grad = jnp.stack(taps).reshape(3, 3, 3, F, C) / jnp.sqrt(jnp.float32(NZ * H * W))
    return (output, input_grad, kernel_grad)
```

```python
import functools
import math

import jax
import jax.numpy as jnp
from jax import lax
from jax.experimental import pallas as pl
from jax.experimental.pallas import tpu as pltpu
from jax.sharding import PartitionSpec as P

W = 16
MESH = pl.DeviceIdType.MESH


def shifted_copies(t, store):
    cells = t.shape[0]
    column = lax.broadcasted_iota(jnp.int32, t.shape, 0) % W
    store(0, jnp.where(column >= 1, pltpu.roll(t, 1, 0), 0.0).astype(jnp.bfloat16))
    store(1, t.astype(jnp.bfloat16))
    store(2, jnp.where(column <= W - 2, pltpu.roll(t, cells - 1, 0), 0.0).astype(jnp.bfloat16))


def kernel(
    sizes, act_ref, w_hbm, grad_ref, out_ref, ig_ref, acc,
    actg, gradg, wide, gwide, w, wf, facc, bacc, fpart, bpart, frecv, brecv,
    w_sem, wf_sem, az_send, ay_send, ax_send, gz_send, gy_send, gc_send,
    a_recv, g_recv, f_send, f_recv, b_send, b_recv,
):
    S, NX, NZ, NY = sizes
    cb, cells = act_ref.shape[1:]
    filters, half = grad_ref.shape[1:]
    chans = NX * cb
    s = lax.axis_index("space")
    c = lax.axis_index("chan")
    x = lax.axis_index("filt")
    z, y = s // NY, s % NY
    oy = 1 - y
    f32, bf16 = jnp.float32, jnp.bfloat16

    def remote(src, dst, send, recv, device):
        return pltpu.make_async_remote_copy(
            src_ref=src, dst_ref=dst, send_sem=send, recv_sem=recv,
            device_id=device, device_id_type=MESH,
        )

    def signal(device):
        pl.semaphore_signal(barrier, inc=1, device_id=device, device_id_type=MESH)

    def a_slot(plane, part):
        return actg.at[plane, pl.ds(pl.multiple_of(part * cb, cb), cb), :]

    def g_slot(plane, part):
        return gradg.at[plane + 1, :, pl.ds(pl.multiple_of(part * half, half), half)]

    ypeer = {"space": z * NY + oy}
    xpeers = [{"filt": (x + e) % NX} for e in range(1, NX)]
    cpeer = {"chan": 1 - c}

    def a_copy(plane, send, device):
        slot = a_slot(plane, x)
        return remote(slot, slot, send, a_recv.at[plane * NX + x], device)

    def g_copy(plane, send, device):
        slot = g_slot(plane, c)
        return remote(slot, slot, send, g_recv.at[plane * 2 + c], device)

    def a_wait(plane, part):
        slot = a_slot(plane, part)
        remote(slot, slot, ay_send.at[0], a_recv.at[plane * NX + part], ypeer).wait_recv()

    def g_wait(plane, part):
        slot = g_slot(plane, part)
        remote(slot, slot, gy_send.at[0], g_recv.at[plane * 2 + part], ypeer).wait_recv()

    def a_z(zz, way):
        to = {"space": (z + way) * NY + y}
        return a_copy(zz * NY + y, az_send.at[(way + 1) // 2 * NZ + zz], to)

    def g_z(zz, way):
        to = {"space": (z + way) * NY + y}
        return g_copy(zz * NY + y, gz_send.at[(way + 1) // 2 * NZ + zz], to)

    def a_y(zz):
        return a_copy(zz * NY + y, ay_send.at[zz], ypeer)

    def g_y(zz):
        return g_copy(zz * NY + y, gy_send.at[zz], ypeer)

    def a_x(plane, e):
        return a_copy(plane, ax_send.at[plane * (NX - 1) + e - 1], xpeers[e - 1])

    def g_c(plane):
        return g_copy(plane, gc_send.at[plane], cpeer)

    def start_x(plane):
        for e in range(1, NX):
            a_x(plane, e).start()

    def inside(zz):
        return (zz >= 0) & (zz < NZ)

    def at_distance(d, run):
        @pl.when(inside(z - d))
        def _():
            run(z - d, -1)

        @pl.when((d > 0) & inside(z + d))
        def _():
            run(z + d, 1)

    actg[s, pl.ds(pl.multiple_of(x * cb, cb), cb), :] = act_ref[0]
    gradg[s + 1, :, pl.ds(pl.multiple_of(c * half, half), half)] = grad_ref[0]
    barrier = pltpu.get_barrier_semaphore()
    for way in (-1, 1):
        @pl.when(inside(z + way))
        def _():
            signal({"space": (z + way) * NY + y})
    for peer in [ypeer, cpeer] + xpeers:
        signal(peer)
    beside = (z + NZ - 1) // NZ + (2 * NZ - 2 - z) // NZ
    pl.semaphore_wait(barrier, NX + 1 + beside)

    for way in (-1, 1):
        @pl.when(inside(z + way))
        def _():
            a_z(z, way).start()
    a_y(z).start()
    start_x(s)
    for way in (-1, 1):
        @pl.when(inside(z + way))
        def _():
            g_z(z, way).start()
    g_y(z).start()
    g_c(s).start()
    w_copy = pltpu.make_async_copy(w_hbm, w, w_sem)
    w_copy.start()

    def wf_copy(i):
        a, b, k = i // 9, i // 3 % 3, i % 3
        return pltpu.make_async_copy(
            w_hbm.at[a, b, k], wf.at[a, b, :, k * chans : (k + 1) * chans], wf_sem.at[i]
        )

    for i in range(27):
        wf_copy(i).start()

    for end in (0, S + 1):
        gradg[end] = jnp.zeros((filters, cells), bf16)
        wide[end] = jnp.zeros(wide.shape[1:], bf16)

    @pl.loop(1, S + 1)
    def _(j):
        wide[j, 0:W, :] = jnp.zeros((W, 3 * chans), bf16)
        wide[j, W + cells : 2 * W + cells, :] = jnp.zeros((W, 3 * chans), bf16)

    for j in range(3):
        gwide[j, 0:W, :] = jnp.zeros((W, gwide.shape[2]), bf16)
        gwide[j, W + cells : 2 * W + cells, :] = jnp.zeros((W, gwide.shape[2]), bf16)

    @pl.loop(0, 27)
    def _(i):
        acc[i // 9, i // 3 % 3, i % 3] = jnp.zeros((filters, chans), f32)

    facc[...] = jnp.zeros_like(facc)
    bacc[...] = jnp.zeros_like(bacc)
    w_copy.wait()
    for i in range(27):
        wf_copy(i).wait()

    lanes = gwide.shape[2] // 3

    def b_copy(e):
        to = (x + e) % NX
        return remote(
            bpart.at[pl.ds(pl.multiple_of(to * cb, cb), cb), :],
            brecv.at[e - 1], b_send.at[e - 1], b_recv.at[e - 1], xpeers[e - 1],
        )

    f_copy = remote(
        fpart.at[:, pl.ds(pl.multiple_of((1 - c) * half, half), half)], frecv, f_send, f_recv, cpeer
    )

    def window(plane, b):
        return wide[plane + 1, pl.ds(pl.multiple_of(b * W, W), cells), :]

    def backward():
        @pl.loop(0, 3)
        def _(j):
            def store(k, value):
                at = (2 - k) * lanes
                gwide[j, W : W + cells, at : at + filters] = value

            shifted_copies(gradg[s + j].astype(f32).T, store)

        @pl.loop(0, 3)
        def _(a):
            total = None
            for b in range(3):
                rows = slice((2 - b) * W, (2 - b) * W + cells)
                if lanes == filters:
                    taps = w[a, b].reshape(3 * filters, chans)
                    terms = [jnp.dot(gwide[2 - a, rows, :], taps, preferred_element_type=f32)]
                else:
                    terms = [
                        jnp.dot(
                            gwide[2 - a, rows, k * lanes : k * lanes + filters],
                            w[a, b, k], preferred_element_type=f32,
                        )
                        for k in range(3)
                    ]
                for term in terms:
                    total = term if total is None else total + term
            bacc[...] += total

        bpart[...] = bacc[...].T

    def send_backward():
        for e in range(1, NX):
            b_copy(e).start()

    def forward():
        @pl.loop(0, 3)
        def _(a):
            total = None
            for b in range(3):
                term = lax.dot_general(
                    window(s + a - 1, b), wf[a, b], (((1,), (1,)), ((), ())), preferred_element_type=f32
                )
                total = term if total is None else total + term
            facc[...] += total

        fpart[...] = facc[...].T
        f_copy.start()

    def prepare(zz):
        @pl.loop(0, NY)
        def _(i):
            plane = zz * NY + i
            for e in range(1, NX):
                a_wait(plane, (x + e) % NX)

            def store(k, value):
                wide[plane + 1, W : W + cells, k * chans : (k + 1) * chans] = value

            shifted_copies(actg[plane].astype(f32).T, store)

    scale = 1.0 / math.sqrt(S * cells)

    def add(a, b, value):
        for k in range(3):
            acc[a, b, k] += value[:, k * chans : (k + 1) * chans] * scale

    def in_pair(zz):
        @pl.loop(0, 3)
        def _(b):
            j = zz * NY
            grads = gradg[pl.ds(j + 1, 2)].reshape(2 * filters, cells)
            low = jnp.dot(grads, window(j, b), preferred_element_type=f32)
            high = jnp.dot(grads, window(j + 1, b), preferred_element_type=f32)
            add(0, b, low[filters:])
            add(1, b, low[:filters] + high[filters:])
            add(2, b, high[:filters])

    def across_pairs(zz):
        @pl.loop(0, 3)
        def _(b):
            j = zz * NY + 1
            add(0, b, jnp.dot(gradg[j + 2], window(j, b), preferred_element_type=f32))
            add(2, b, jnp.dot(gradg[j + 1], window(j + 1, b), preferred_element_type=f32))

    def filter_grad(zz, way):
        prepare(zz)
        in_pair(zz)

        @pl.when(zz != z)
        def _():
            across_pairs(zz + (-1 - way) // 2)

    def relay(zz, way, wait, along, across, last):
        plane = zz * NY + y
        wait(plane)

        @pl.when(inside(z - way))
        def _():
            along(zz, -way).start()

        across(zz).start()
        last(plane)

    def pass_on(zz, wait, last):
        plane = zz * NY + oy
        wait(plane)
        last(plane)

    def a_own(plane):
        a_wait(plane, x)

    def g_own(plane):
        g_wait(plane, c)

    def start_c(plane):
        g_c(plane).start()

    def core_halves(zz, way):
        for n in range(NY):
            g_wait(zz * NY + n, 1 - c)

    @pl.loop(1, NZ + 2)
    def _(d):
        at_distance(d - 1, lambda zz, way: pass_on(zz, a_own, start_x))
        at_distance(d, lambda zz, way: relay(zz, way, a_own, a_z, a_y, start_x))
        at_distance(d - 1, lambda zz, way: pass_on(zz, g_own, start_c))
        at_distance(d, lambda zz, way: relay(zz, way, g_own, g_z, g_y, start_c))
        at_distance(d - 1, core_halves)

        @pl.when(d == 2)
        def _():
            backward()

        @pl.when(d == 4)
        def _():
            send_backward()
            forward()

        @pl.when(d != 2)
        def _():
            at_distance(jnp.maximum(d - 2, 0), filter_grad)

    f_copy.wait()
    out_ref[0] = (fpart[:, pl.ds(pl.multiple_of(c * half, half), half)] + frecv[...]).astype(bf16)
    own = bpart[pl.ds(pl.multiple_of(x * cb, cb), cb), :]
    for e in range(1, NX):
        b_copy(e).wait()
        own = own + brecv[e - 1]
    ig_ref[0] = own.astype(bf16)

    @pl.loop(0, NZ)
    def _(zz):
        for way in (-1, 1):
            @pl.when(inside(z + way) & ((z - zz) * way >= 0))
            def _():
                a_z(zz, way).wait_send()
                g_z(zz, way).wait_send()
        a_y(zz).wait_send()
        g_y(zz).wait_send()

    @pl.loop(0, S)
    def _(plane):
        for e in range(1, NX):
            a_x(plane, e).wait_send()
        g_c(plane).wait_send()


def body(activation, weights, out_grad):
    S = lax.axis_size("space")
    NX = lax.axis_size("filt")
    NY = 2
    NZ = S // NY
    cb, cells = activation.shape[1:]
    filters, half = out_grad.shape[1:]
    chans = NX * cb
    bf16, f32 = jnp.bfloat16, jnp.float32
    dma = pltpu.SemaphoreType.DMA
    vmem = pl.BlockSpec(memory_space=pltpu.VMEM)
    hbm = pl.BlockSpec(memory_space=pl.ANY)
    shapes = ((out_grad.shape, bf16), (activation.shape, bf16), (weights.shape, f32))
    results = pl.pallas_call(
        functools.partial(kernel, (S, NX, NZ, NY)),
        out_shape=tuple(pltpu.VMEM(*shape) for shape in shapes),
        in_specs=[vmem, hbm, vmem],
        out_specs=(vmem, vmem, vmem),
        scratch_shapes=[
            pltpu.VMEM((S, chans, cells), bf16),
            pltpu.VMEM((S + 2, filters, cells), bf16),
            pltpu.VMEM((S + 2, cells + 2 * W, 3 * chans), bf16),
            pltpu.VMEM((3, cells + 2 * W, 3 * pl.cdiv(filters, 128) * 128), bf16),
            pltpu.VMEM(weights.shape, bf16),
            pltpu.VMEM((3, 3, filters, 3 * chans), bf16),
            pltpu.VMEM((cells, filters), f32),
            pltpu.VMEM((cells, chans), f32),
            pltpu.VMEM((filters, cells), f32),
            pltpu.VMEM((chans, cells), f32),
            pltpu.VMEM((filters, half), f32),
            pltpu.VMEM((NX - 1, cb, cells), f32),
            dma, dma((27,)),
            dma((2 * NZ,)), dma((NZ,)), dma((S * (NX - 1),)),
            dma((2 * NZ,)), dma((NZ,)), dma((S,)),
            dma((S * NX,)), dma((S * 2,)),
            dma, dma, dma((NX - 1,)), dma((NX - 1,)),
        ],
        compiler_params=pltpu.CompilerParams(
            collective_id=0, has_side_effects=True, vmem_limit_bytes=50 * 1024 * 1024
        ),
    )(activation, weights, out_grad)
    return results


def near_kernel(
    act_hbm, w_hbm, grad_hbm, out_ref, ig_ref, acc,
    actg, gradg, wide, gwide, w, wf, facc, bacc, fpart, bpart, frecv, brecv,
    in_sem, w_sem, az_send, ay_send, ax_send, gz_send, gy_send, gc_send,
    a_recv, g_recv, f_send, f_recv, b_send, b_recv,
):
    NY, NZ, H = 2, 4, 2
    S = NY * NZ
    cb, cells = act_hbm.shape[1:]
    filters, half = grad_hbm.shape[1:]
    chans = 2 * cb
    a_rows, g_rows = cb // H, filters // H
    s = lax.axis_index("space")
    c = lax.axis_index("chan")
    x = lax.axis_index("filt")
    z, y = s // NY, s % NY
    oy = 1 - y
    f32, bf16 = jnp.float32, jnp.bfloat16
    ypeer = {"space": z * NY + oy}
    xpeer = {"filt": 1 - x}
    cpeer = {"chan": 1 - c}

    def zpeer(way):
        return {"space": (z + way) * NY + y}

    def inside(zz):
        return (zz >= 0) & (zz < NZ)

    def remote(src, dst, send, recv, device):
        return pltpu.make_async_remote_copy(
            src_ref=src, dst_ref=dst, send_sem=send, recv_sem=recv,
            device_id=device, device_id_type=MESH,
        )

    def a_slot(plane, part, h):
        return actg.at[plane, pl.ds(pl.multiple_of(part * cb + h * a_rows, a_rows), a_rows), :]

    def g_slot(plane, part, h):
        return gradg.at[plane, pl.ds(h * g_rows, g_rows), pl.ds(pl.multiple_of(part * half, half), half)]

    def a_copy(plane, h, send, device):
        slot = a_slot(plane, x, h)
        return remote(slot, slot, send, a_recv.at[plane * 2 + x, h], device)

    def g_copy(plane, h, send, device):
        slot = g_slot(plane, c, h)
        return remote(slot, slot, send, g_recv.at[plane * 2 + c, h], device)

    def a_z(zz, way, h):
        return a_copy(zz * NY + y, h, az_send.at[(way + 1) // 2 * NZ + zz, h], zpeer(way))

    def g_z(zz, way, h):
        return g_copy(zz * NY + y, h, gz_send.at[(way + 1) // 2 * NZ + zz, h], zpeer(way))

    def a_y(zz, h):
        return a_copy(zz * NY + y, h, ay_send.at[zz, h], ypeer)

    def g_y(zz, h):
        return g_copy(zz * NY + y, h, gy_send.at[zz, h], ypeer)

    def a_x(plane, h):
        return a_copy(plane, h, ax_send.at[plane, h], xpeer)

    def g_c(plane, h):
        return g_copy(plane, h, gc_send.at[plane, h], cpeer)

    def a_wait(plane, part, h):
        slot = a_slot(plane, part, h)
        remote(slot, slot, ax_send.at[0, 0], a_recv.at[plane * 2 + part, h], xpeer).wait_recv()

    def g_wait(plane, part, h):
        slot = g_slot(plane, part, h)
        remote(slot, slot, gc_send.at[0, 0], g_recv.at[plane * 2 + part, h], cpeer).wait_recv()

    own_a = pltpu.make_async_copy(
        act_hbm.at[0], actg.at[s, pl.ds(pl.multiple_of(x * cb, cb), cb), :], in_sem.at[0]
    )
    own_g = pltpu.make_async_copy(
        grad_hbm.at[0], gradg.at[s, :, pl.ds(pl.multiple_of(c * half, half), half)], in_sem.at[1]
    )
    own_a.start()
    own_g.start()
    barrier = pltpu.get_barrier_semaphore()

    def signal(device):
        pl.semaphore_signal(barrier, inc=1, device_id=device, device_id_type=MESH)

    for way in (-1, 1):
        @pl.when(inside(z + way))
        def _():
            signal(zpeer(way))
    for peer in (ypeer, cpeer, xpeer):
        signal(peer)
    w_copy = pltpu.make_async_copy(w_hbm, w, w_sem.at[27])
    w_copy.start()

    def wf_copy(i):
        a, b, k = i // 9, i // 3 % 3, i % 3
        return pltpu.make_async_copy(
            w_hbm.at[a, b, k], wf.at[a, b, :, k * chans : (k + 1) * chans], w_sem.at[i]
        )

    for i in range(27):
        wf_copy(i).start()

    @pl.loop(0, S)
    def _(j):
        wide[j, 0:W, :] = jnp.zeros((W, 3 * chans), bf16)
        wide[j, W + cells : 2 * W + cells, :] = jnp.zeros((W, 3 * chans), bf16)

    for j in range(3):
        gwide[j, 0:W, :] = jnp.zeros((W, 3 * filters), bf16)
        gwide[j, W + cells : 2 * W + cells, :] = jnp.zeros((W, 3 * filters), bf16)

    @pl.loop(0, 27)
    def _(i):
        acc[i // 9, i // 3 % 3, i % 3] = jnp.zeros((filters, chans), f32)

    own_a.wait()
    own_g.wait()
    pl.semaphore_wait(barrier, 3 + (z + NZ - 1) // NZ + (2 * NZ - 2 - z) // NZ)

    for h in range(H):
        for way in (-1, 1):
            @pl.when(inside(z + way))
            def _():
                a_z(z, way, h).start()
        a_y(z, h).start()
        a_x(s, h).start()
        for way in (-1, 1):
            @pl.when(inside(z + way))
            def _():
                g_z(z, way, h).start()
        g_y(z, h).start()
        g_c(s, h).start()

    def from_z(d, wait, part, along, others):
        for way in (-1, 1):
            zz = z + way * d

            @pl.when(inside(zz))
            def _():
                plane = zz * NY + y
                for h in range(H):
                    wait(plane, part, h)

                    @pl.when(inside(z - way))
                    def _():
                        along(zz, -way, h).start()

                    others(zz, plane, h)

    def a_others(zz, plane, h):
        a_y(zz, h).start()
        a_x(plane, h).start()

    def g_others(zz, plane, h):
        g_y(zz, h).start()
        g_c(plane, h).start()

    def a_from_z(d):
        from_z(d, a_wait, x, a_z, a_others)

    def g_from_z(d):
        from_z(d, g_wait, c, g_z, g_others)

    def a_from_y(zz):
        for h in range(H):
            a_wait(zz * NY + oy, x, h)
            a_x(zz * NY + oy, h).start()

    def g_from_y(zz):
        for h in range(H):
            g_wait(zz * NY + oy, c, h)
            g_c(zz * NY + oy, h).start()

    def a_rest(plane):
        for h in range(H):
            a_wait(plane, 1 - x, h)

    def g_rest(plane):
        for h in range(H):
            g_wait(plane, 1 - c, h)

    def window(plane, b):
        return wide[plane, b * W : b * W + cells, :]

    def prepare(plane):
        def store(k, value):
            wide[plane, W : W + cells, k * chans : (k + 1) * chans] = value

        shifted_copies(actg[plane].astype(f32).T, store)

    scale = 1.0 / math.sqrt(S * cells)

    def add(a, b, value):
        for k in range(3):
            acc[a, b, k] += value[:, k * chans : (k + 1) * chans] * scale

    def block(wp, gp):
        grad = gradg[gp]
        for b in range(3):
            add(wp - gp + 1, b, jnp.dot(grad, window(wp, b), preferred_element_type=f32))

    def in_pair(wp, zz):
        grads = gradg[pl.ds(zz * NY, NY)].reshape(NY * filters, cells)
        at = wp - zz * NY
        for b in range(3):
            value = jnp.dot(grads, window(wp, b), preferred_element_type=f32)
            add(at + 1, b, value[:filters])
            add(at, b, value[filters:])

    def backward(j, plane):
        def store(k, value):
            at = (2 - k) * filters
            gwide[j, W : W + cells, at : at + filters] = value

        shifted_copies(gradg[plane].astype(f32).T, store)
        a = s + 1 - plane
        total = None
        for b in range(3):
            rows = slice((2 - b) * W, (2 - b) * W + cells)
            taps = w[a, b].reshape(3 * filters, chans)
            term = jnp.dot(gwide[j, rows, :], taps, preferred_element_type=f32)
            total = term if total is None else total + term
        bacc[...] = total if j == 0 else bacc[...] + total

    def forward(j, plane):
        a = plane - s + 1
        total = None
        for b in range(3):
            term = lax.dot_general(
                window(plane, b), wf[a, b], (((1,), (1,)), ((), ())), preferred_element_type=f32
            )
            total = term if total is None else total + term
        facc[...] = total if j == 0 else facc[...] + total

    b_copy = remote(
        bpart.at[pl.ds(pl.multiple_of((1 - x) * cb, cb), cb), :], brecv, b_send, b_recv, xpeer
    )
    f_copy = remote(
        fpart.at[:, pl.ds(pl.multiple_of((1 - c) * half, half), half)], frecv, f_send, f_recv, cpeer
    )
    side = 2 * y - 1
    third = s + side

    def order(o):
        end = jnp.where(z == 0, o, NZ - 1 - o)
        last = jnp.where(z == 1, NZ - 1, 0)
        mid = jnp.where(o == 1, z + side, jnp.where(o == 2, z - side, jnp.where(o == 3, last, z)))
        return jnp.where((z == 0) | (z == NZ - 1), end, mid)

    other = z * NY + oy
    w_copy.wait()
    g_rest(s)
    backward(0, s)
    a_from_y(z)
    a_from_z(1)
    for i in range(27):
        wf_copy(i).wait()
    a_rest(s)
    prepare(s)
    block(s, s)
    g_from_y(z)
    g_from_z(1)
    forward(0, s)
    g_rest(other)
    backward(1, other)
    a_from_y(order(1))
    a_from_z(2)
    block(s, other)
    a_rest(other)
    prepare(other)
    in_pair(other, z)
    g_from_y(order(1))
    g_from_z(2)
    forward(1, other)

    @pl.loop(1, NZ)
    def _(o):
        zz = order(o)
        nxt = order(jnp.minimum(o + 1, NZ - 1))
        mine, theirs = zz * NY + y, zz * NY + oy
        a_rest(mine)
        prepare(mine)
        g_rest(mine)
        g_rest(theirs)
        in_pair(mine, zz)

        @pl.when(o < NZ - 1)
        def _():
            a_from_y(nxt)

        @pl.when(o < NZ - 2)
        def _():
            a_from_z(o + 2)

        a_rest(theirs)
        prepare(theirs)
        in_pair(theirs, zz)

        @pl.when(o < NZ - 1)
        def _():
            g_from_y(nxt)

        @pl.when(o < NZ - 2)
        def _():
            g_from_z(o + 2)

        low = jnp.where(zz > z, zz * NY - 1, zz * NY + NY - 1)
        block(low, low + 1)
        block(low + 1, low)

        @pl.when(o == 1)
        def _():
            @pl.when((third >= 0) & (third < S))
            def _():
                backward(2, third)
                forward(2, third)

            bpart[...] = bacc[...].T
            fpart[...] = facc[...].T
            f_copy.start()

        @pl.when(o == 2)
        def _():
            b_copy.start()

    f_copy.wait()
    out_ref[0] = (fpart[:, pl.ds(pl.multiple_of(c * half, half), half)] + frecv[...]).astype(bf16)
    b_copy.wait()
    ig_ref[0] = (bpart[pl.ds(pl.multiple_of(x * cb, cb), cb), :] + brecv[...]).astype(bf16)

    @pl.loop(0, NZ)
    def _(zz):
        for h in range(H):
            for way in (-1, 1):
                @pl.when(inside(z + way) & ((z - zz) * way >= 0))
                def _():
                    a_z(zz, way, h).wait_send()
                    g_z(zz, way, h).wait_send()
            a_y(zz, h).wait_send()
            g_y(zz, h).wait_send()

    @pl.loop(0, S)
    def _(plane):
        for h in range(H):
            a_x(plane, h).wait_send()
            g_c(plane, h).wait_send()


def near_body(activation, weights, out_grad):
    S = lax.axis_size("space")
    NY, H = 2, 2
    NZ = S // NY
    cb, cells = activation.shape[1:]
    filters, half = out_grad.shape[1:]
    chans = 2 * cb
    bf16, f32 = jnp.bfloat16, jnp.float32
    dma = pltpu.SemaphoreType.DMA
    vmem = pl.BlockSpec(memory_space=pltpu.VMEM)
    hbm = pl.BlockSpec(memory_space=pl.ANY)
    shapes = ((out_grad.shape, bf16), (activation.shape, bf16), (weights.shape, f32))
    return pl.pallas_call(
        near_kernel,
        out_shape=tuple(pltpu.VMEM(*shape) for shape in shapes),
        in_specs=[hbm, hbm, hbm],
        out_specs=(vmem, vmem, vmem),
        scratch_shapes=[
            pltpu.VMEM((S, chans, cells), bf16),
            pltpu.VMEM((S, filters, cells), bf16),
            pltpu.VMEM((S, cells + 2 * W, 3 * chans), bf16),
            pltpu.VMEM((3, cells + 2 * W, 3 * filters), bf16),
            pltpu.VMEM(weights.shape, bf16),
            pltpu.VMEM((3, 3, filters, 3 * chans), bf16),
            pltpu.VMEM((cells, filters), f32),
            pltpu.VMEM((cells, chans), f32),
            pltpu.VMEM((filters, cells), f32),
            pltpu.VMEM((chans, cells), f32),
            pltpu.VMEM((filters, half), f32),
            pltpu.VMEM((cb, cells), f32),
            dma((2,)), dma((28,)),
            dma((2 * NZ, H)), dma((NZ, H)), dma((S, H)),
            dma((2 * NZ, H)), dma((NZ, H)), dma((S, H)),
            dma((S * 2, H)), dma((S * 2, H)),
            dma, dma, dma, dma,
        ],
        compiler_params=pltpu.CompilerParams(
            collective_id=1, has_side_effects=True, vmem_limit_bytes=50 * 1024 * 1024
        ),
    )(activation, weights, out_grad)


def solution(mesh):
    placed = (
        P("space", ("chan", "filt"), None),
        P(None, None, None, "filt", "chan"),
        P("space", "filt", "chan"),
    )
    near = mesh.shape["space"] == 8 and mesh.shape["filt"] == 2 and mesh.shape["chan"] == 2
    return jax.shard_map(
        near_body if near else body,
        mesh=mesh,
        in_specs=placed,
        out_specs=(
            P("space", "filt", "chan"),
            P("space", ("chan", "filt"), None),
            P(None, None, None, "filt", "chan"),
        ),
        check_vma=False,
    )
```

```python
import functools
import math

import jax
import jax.numpy as jnp
from jax import lax
from jax.experimental import pallas as pl
from jax.experimental.pallas import tpu as pltpu
from jax.sharding import PartitionSpec as P

W = 16
MESH = pl.DeviceIdType.MESH


def shifted_copies(t, store):
    cells = t.shape[0]
    column = lax.broadcasted_iota(jnp.int32, t.shape, 0) % W
    store(0, jnp.where(column >= 1, pltpu.roll(t, 1, 0), 0.0).astype(jnp.bfloat16))
    store(1, t.astype(jnp.bfloat16))
    store(2, jnp.where(column <= W - 2, pltpu.roll(t, cells - 1, 0), 0.0).astype(jnp.bfloat16))


def kernel(
    sizes, act_ref, w_hbm, grad_ref, out_ref, ig_ref, acc,
    actg, gradg, wide, gwide, w, wf, facc, bacc, fpart, bpart, frecv, brecv,
    w_sem, wf_sem, az_send, ay_send, ax_send, gz_send, gy_send, gc_send,
    a_recv, g_recv, f_send, f_recv, b_send, b_recv,
):
    S, NX, NZ, NY = sizes
    cb, cells = act_ref.shape[1:]
    filters, half = grad_ref.shape[1:]
    chans = NX * cb
    s = lax.axis_index("space")
    c = lax.axis_index("chan")
    x = lax.axis_index("filt")
    z, y = s // NY, s % NY
    oy = 1 - y
    f32, bf16 = jnp.float32, jnp.bfloat16

    def remote(src, dst, send, recv, device):
        return pltpu.make_async_remote_copy(
            src_ref=src, dst_ref=dst, send_sem=send, recv_sem=recv,
            device_id=device, device_id_type=MESH,
        )

    def signal(device):
        pl.semaphore_signal(barrier, inc=1, device_id=device, device_id_type=MESH)

    def a_slot(plane, part):
        return actg.at[plane, pl.ds(pl.multiple_of(part * cb, cb), cb), :]

    def g_slot(plane, part):
        return gradg.at[plane + 1, :, pl.ds(pl.multiple_of(part * half, half), half)]

    ypeer = {"space": z * NY + oy}
    xpeers = [{"filt": (x + e) % NX} for e in range(1, NX)]
    cpeer = {"chan": 1 - c}

    def a_copy(plane, send, device):
        slot = a_slot(plane, x)
        return remote(slot, slot, send, a_recv.at[plane * NX + x], device)

    def g_copy(plane, send, device):
        slot = g_slot(plane, c)
        return remote(slot, slot, send, g_recv.at[plane * 2 + c], device)

    def a_wait(plane, part):
        slot = a_slot(plane, part)
        remote(slot, slot, ay_send.at[0], a_recv.at[plane * NX + part], ypeer).wait_recv()

    def g_wait(plane, part):
        slot = g_slot(plane, part)
        remote(slot, slot, gy_send.at[0], g_recv.at[plane * 2 + part], ypeer).wait_recv()

    def a_z(zz, way):
        to = {"space": (z + way) * NY + y}
        return a_copy(zz * NY + y, az_send.at[(way + 1) // 2 * NZ + zz], to)

    def g_z(zz, way):
        to = {"space": (z + way) * NY + y}
        return g_copy(zz * NY + y, gz_send.at[(way + 1) // 2 * NZ + zz], to)

    def a_y(zz):
        return a_copy(zz * NY + y, ay_send.at[zz], ypeer)

    def g_y(zz):
        return g_copy(zz * NY + y, gy_send.at[zz], ypeer)

    def a_x(plane, e):
        return a_copy(plane, ax_send.at[plane * (NX - 1) + e - 1], xpeers[e - 1])

    def g_c(plane):
        return g_copy(plane, gc_send.at[plane], cpeer)

    def start_x(plane):
        for e in range(1, NX):
            a_x(plane, e).start()

    def inside(zz):
        return (zz >= 0) & (zz < NZ)

    def at_distance(d, run):
        @pl.when(inside(z - d))
        def _():
            run(z - d, -1)

        @pl.when((d > 0) & inside(z + d))
        def _():
            run(z + d, 1)

    actg[s, pl.ds(pl.multiple_of(x * cb, cb), cb), :] = act_ref[0]
    gradg[s + 1, :, pl.ds(pl.multiple_of(c * half, half), half)] = grad_ref[0]
    barrier = pltpu.get_barrier_semaphore()
    for way in (-1, 1):
        @pl.when(inside(z + way))
        def _():
            signal({"space": (z + way) * NY + y})
    for peer in [ypeer, cpeer] + xpeers:
        signal(peer)
    beside = (z + NZ - 1) // NZ + (2 * NZ - 2 - z) // NZ
    pl.semaphore_wait(barrier, NX + 1 + beside)

    for way in (-1, 1):
        @pl.when(inside(z + way))
        def _():
            a_z(z, way).start()
    a_y(z).start()
    start_x(s)
    for way in (-1, 1):
        @pl.when(inside(z + way))
        def _():
            g_z(z, way).start()
    g_y(z).start()
    g_c(s).start()
    w_copy = pltpu.make_async_copy(w_hbm, w, w_sem)
    w_copy.start()

    def wf_copy(i):
        a, b, k = i // 9, i // 3 % 3, i % 3
        return pltpu.make_async_copy(
            w_hbm.at[a, b, k], wf.at[a, b, :, k * chans : (k + 1) * chans], wf_sem.at[i]
        )

    for i in range(27):
        wf_copy(i).start()

    for end in (0, S + 1):
        gradg[end] = jnp.zeros((filters, cells), bf16)
        wide[end] = jnp.zeros(wide.shape[1:], bf16)

    @pl.loop(1, S + 1)
    def _(j):
        wide[j, 0:W, :] = jnp.zeros((W, 3 * chans), bf16)
        wide[j, W + cells : 2 * W + cells, :] = jnp.zeros((W, 3 * chans), bf16)

    for j in range(3):
        gwide[j, 0:W, :] = jnp.zeros((W, gwide.shape[2]), bf16)
        gwide[j, W + cells : 2 * W + cells, :] = jnp.zeros((W, gwide.shape[2]), bf16)

    @pl.loop(0, 27)
    def _(i):
        acc[i // 9, i // 3 % 3, i % 3] = jnp.zeros((filters, chans), f32)

    facc[...] = jnp.zeros_like(facc)
    bacc[...] = jnp.zeros_like(bacc)
    w_copy.wait()
    for i in range(27):
        wf_copy(i).wait()

    lanes = gwide.shape[2] // 3

    def b_copy(e):
        to = (x + e) % NX
        return remote(
            bpart.at[pl.ds(pl.multiple_of(to * cb, cb), cb), :],
            brecv.at[e - 1], b_send.at[e - 1], b_recv.at[e - 1], xpeers[e - 1],
        )

    f_copy = remote(
        fpart.at[:, pl.ds(pl.multiple_of((1 - c) * half, half), half)], frecv, f_send, f_recv, cpeer
    )

    def window(plane, b):
        return wide[plane + 1, pl.ds(pl.multiple_of(b * W, W), cells), :]

    def backward():
        @pl.loop(0, 3)
        def _(j):
            def store(k, value):
                at = (2 - k) * lanes
                gwide[j, W : W + cells, at : at + filters] = value

            shifted_copies(gradg[s + j].astype(f32).T, store)

        @pl.loop(0, 3)
        def _(a):
            total = None
            for b in range(3):
                rows = slice((2 - b) * W, (2 - b) * W + cells)
                if lanes == filters:
                    taps = w[a, b].reshape(3 * filters, chans)
                    terms = [jnp.dot(gwide[2 - a, rows, :], taps, preferred_element_type=f32)]
                else:
                    terms = [
                        jnp.dot(
                            gwide[2 - a, rows, k * lanes : k * lanes + filters],
                            w[a, b, k], preferred_element_type=f32,
                        )
                        for k in range(3)
                    ]
                for term in terms:
                    total = term if total is None else total + term
            bacc[...] += total

        bpart[...] = bacc[...].T

    def send_backward():
        for e in range(1, NX):
            b_copy(e).start()

    def forward():
        @pl.loop(0, 3)
        def _(a):
            total = None
            for b in range(3):
                term = lax.dot_general(
                    window(s + a - 1, b), wf[a, b], (((1,), (1,)), ((), ())), preferred_element_type=f32
                )
                total = term if total is None else total + term
            facc[...] += total

        fpart[...] = facc[...].T
        f_copy.start()

    def prepare(zz):
        @pl.loop(0, NY)
        def _(i):
            plane = zz * NY + i
            for e in range(1, NX):
                a_wait(plane, (x + e) % NX)

            def store(k, value):
                wide[plane + 1, W : W + cells, k * chans : (k + 1) * chans] = value

            shifted_copies(actg[plane].astype(f32).T, store)

    scale = 1.0 / math.sqrt(S * cells)

    def add(a, b, value):
        for k in range(3):
            acc[a, b, k] += value[:, k * chans : (k + 1) * chans] * scale

    def in_pair(zz):
        @pl.loop(0, 3)
        def _(b):
            j = zz * NY
            grads = gradg[pl.ds(j + 1, 2)].reshape(2 * filters, cells)
            low = jnp.dot(grads, window(j, b), preferred_element_type=f32)
            high = jnp.dot(grads, window(j + 1, b), preferred_element_type=f32)
            add(0, b, low[filters:])
            add(1, b, low[:filters] + high[filters:])
            add(2, b, high[:filters])

    def across_pairs(zz):
        @pl.loop(0, 3)
        def _(b):
            j = zz * NY + 1
            add(0, b, jnp.dot(gradg[j + 2], window(j, b), preferred_element_type=f32))
            add(2, b, jnp.dot(gradg[j + 1], window(j + 1, b), preferred_element_type=f32))

    def filter_grad(zz, way):
        prepare(zz)
        in_pair(zz)

        @pl.when(zz != z)
        def _():
            across_pairs(zz + (-1 - way) // 2)

    def relay(zz, way, wait, along, across, last):
        plane = zz * NY + y
        wait(plane)

        @pl.when(inside(z - way))
        def _():
            along(zz, -way).start()

        across(zz).start()
        last(plane)

    def pass_on(zz, wait, last):
        plane = zz * NY + oy
        wait(plane)
        last(plane)

    def a_own(plane):
        a_wait(plane, x)

    def g_own(plane):
        g_wait(plane, c)

    def start_c(plane):
        g_c(plane).start()

    def core_halves(zz, way):
        for n in range(NY):
            g_wait(zz * NY + n, 1 - c)

    @pl.loop(1, NZ + 2)
    def _(d):
        at_distance(d - 1, lambda zz, way: pass_on(zz, a_own, start_x))
        at_distance(d, lambda zz, way: relay(zz, way, a_own, a_z, a_y, start_x))
        at_distance(d - 1, lambda zz, way: pass_on(zz, g_own, start_c))
        at_distance(d, lambda zz, way: relay(zz, way, g_own, g_z, g_y, start_c))
        at_distance(d - 1, core_halves)

        @pl.when(d == 2)
        def _():
            backward()

        @pl.when(d == 4)
        def _():
            send_backward()
            forward()

        @pl.when(d != 2)
        def _():
            at_distance(jnp.maximum(d - 2, 0), filter_grad)

    f_copy.wait()
    out_ref[0] = (fpart[:, pl.ds(pl.multiple_of(c * half, half), half)] + frecv[...]).astype(bf16)
    own = bpart[pl.ds(pl.multiple_of(x * cb, cb), cb), :]
    for e in range(1, NX):
        b_copy(e).wait()
        own = own + brecv[e - 1]
    ig_ref[0] = own.astype(bf16)

    @pl.loop(0, NZ)
    def _(zz):
        for way in (-1, 1):
            @pl.when(inside(z + way) & ((z - zz) * way >= 0))
            def _():
                a_z(zz, way).wait_send()
                g_z(zz, way).wait_send()
        a_y(zz).wait_send()
        g_y(zz).wait_send()

    @pl.loop(0, S)
    def _(plane):
        for e in range(1, NX):
            a_x(plane, e).wait_send()
        g_c(plane).wait_send()


def body(activation, weights, out_grad):
    S = lax.axis_size("space")
    NX = lax.axis_size("filt")
    NY = 2
    NZ = S // NY
    cb, cells = activation.shape[1:]
    filters, half = out_grad.shape[1:]
    chans = NX * cb
    bf16, f32 = jnp.bfloat16, jnp.float32
    dma = pltpu.SemaphoreType.DMA
    vmem = pl.BlockSpec(memory_space=pltpu.VMEM)
    hbm = pl.BlockSpec(memory_space=pl.ANY)
    shapes = ((out_grad.shape, bf16), (activation.shape, bf16), (weights.shape, f32))
    results = pl.pallas_call(
        functools.partial(kernel, (S, NX, NZ, NY)),
        out_shape=tuple(pltpu.VMEM(*shape) for shape in shapes),
        in_specs=[vmem, hbm, vmem],
        out_specs=(vmem, vmem, vmem),
        scratch_shapes=[
            pltpu.VMEM((S, chans, cells), bf16),
            pltpu.VMEM((S + 2, filters, cells), bf16),
            pltpu.VMEM((S + 2, cells + 2 * W, 3 * chans), bf16),
            pltpu.VMEM((3, cells + 2 * W, 3 * pl.cdiv(filters, 128) * 128), bf16),
            pltpu.VMEM(weights.shape, bf16),
            pltpu.VMEM((3, 3, filters, 3 * chans), bf16),
            pltpu.VMEM((cells, filters), f32),
            pltpu.VMEM((cells, chans), f32),
            pltpu.VMEM((filters, cells), f32),
            pltpu.VMEM((chans, cells), f32),
            pltpu.VMEM((filters, half), f32),
            pltpu.VMEM((NX - 1, cb, cells), f32),
            dma, dma((27,)),
            dma((2 * NZ,)), dma((NZ,)), dma((S * (NX - 1),)),
            dma((2 * NZ,)), dma((NZ,)), dma((S,)),
            dma((S * NX,)), dma((S * 2,)),
            dma, dma, dma((NX - 1,)), dma((NX - 1,)),
        ],
        compiler_params=pltpu.CompilerParams(
            collective_id=0, has_side_effects=True, vmem_limit_bytes=50 * 1024 * 1024
        ),
    )(activation, weights, out_grad)
    return results


def pair_at(z, y, NZ, o):
    side = 2 * y - 1
    out = jnp.where(z == 0, o, NZ - 1 - o)
    last = jnp.where(z == 1, NZ - 1, 0)
    mid = jnp.where(o == 1, z + side, jnp.where(o == 2, z - side, jnp.where(o == 3, last, z)))
    return jnp.where((z == 0) | (z == NZ - 1), out, mid)


def last_kernel(
    out_ref, ig_ref, acc, gradg, wide, out_hbm, ig_hbm, kg_hbm, stage, out_sem, ig_sem, kg_sem
):
    NY, NZ = 2, 4
    S, filters, cells = gradg.shape
    chans = acc.shape[-1]
    s = lax.axis_index("space")
    z, y = s // NY, s % NY
    oy = 1 - y
    f32 = jnp.float32
    out_copy = pltpu.make_async_copy(out_ref, out_hbm, out_sem)
    ig_copy = pltpu.make_async_copy(ig_ref, ig_hbm, ig_sem)
    out_copy.start()
    ig_copy.start()
    zz = pair_at(z, y, NZ, NZ - 1)
    low = jnp.where(zz > z, zz * NY - 1, zz * NY + NY - 1)
    scale = 1.0 / math.sqrt(S * cells)

    def part(value, k):
        return value[:, k * chans : (k + 1) * chans] * scale

    for b in range(3):
        def window(plane):
            return wide[plane, b * W : b * W + cells, :]

        before = jnp.dot(gradg[low + 1], window(low), preferred_element_type=f32)
        after = jnp.dot(gradg[low], window(low + 1), preferred_element_type=f32)
        for k in range(3):
            stage[0, b, k] = acc[0, b, k] + part(before, k)
            stage[1, b, k] = acc[1, b, k]
            stage[2, b, k] = acc[2, b, k] + part(after, k)
        grads = gradg[pl.ds(zz * NY, NY)].reshape(NY * filters, cells)
        value = jnp.dot(grads, window(zz * NY + oy), preferred_element_type=f32)
        for k in range(3):
            stage[oy + 1, b, k] += part(value[:filters], k)
            stage[oy, b, k] += part(value[filters:], k)
        for a in range(3):
            pltpu.make_async_copy(stage.at[a, b], kg_hbm.at[a, b], kg_sem).start()
    out_copy.wait()
    ig_copy.wait()
    pltpu.make_async_copy(stage, kg_hbm, kg_sem).wait()


def near_kernel(
    act_hbm, w_hbm, grad_hbm, out_ref, ig_ref, acc, gradg, wide,
    actg, gwide, w, wf, facc, bacc, fpart, bpart, frecv, brecv,
    in_sem, w_sem, az_send, ay_send, ax_send, gz_send, gy_send, gc_send,
    a_recv, g_recv, f_send, f_recv, b_send, b_recv,
):
    NY, NZ, H, parts = 2, 4, 1, 4
    S = NY * NZ
    cb, cells = act_hbm.shape[1:]
    filters, half = grad_hbm.shape[1:]
    chans = 2 * cb
    a_rows, g_rows = cb // H, filters // H
    s = lax.axis_index("space")
    c = lax.axis_index("chan")
    x = lax.axis_index("filt")
    z, y = s // NY, s % NY
    oy = 1 - y
    f32, bf16 = jnp.float32, jnp.bfloat16
    ypeer = {"space": z * NY + oy}
    xpeer = {"filt": 1 - x}
    cpeer = {"chan": 1 - c}

    def zpeer(way):
        return {"space": (z + way) * NY + y}

    def inside(zz):
        return (zz >= 0) & (zz < NZ)

    def remote(src, dst, send, recv, device):
        return pltpu.make_async_remote_copy(
            src_ref=src, dst_ref=dst, send_sem=send, recv_sem=recv,
            device_id=device, device_id_type=MESH,
        )

    def a_slot(plane, part, h):
        return actg.at[plane, pl.ds(pl.multiple_of(part * cb + h * a_rows, a_rows), a_rows), :]

    def g_slot(plane, part, h):
        return gradg.at[plane, pl.ds(h * g_rows, g_rows), pl.ds(pl.multiple_of(part * half, half), half)]

    def a_copy(plane, h, send, device):
        slot = a_slot(plane, x, h)
        return remote(slot, slot, send, a_recv.at[plane * 2 + x, h], device)

    def g_copy(plane, h, send, device):
        slot = g_slot(plane, c, h)
        return remote(slot, slot, send, g_recv.at[plane * 2 + c, h], device)

    def a_z(zz, way, h):
        return a_copy(zz * NY + y, h, az_send, zpeer(way))

    def g_z(zz, way, h):
        return g_copy(zz * NY + y, h, gz_send, zpeer(way))

    def a_y(zz, h):
        return a_copy(zz * NY + y, h, ay_send, ypeer)

    def g_y(zz, h):
        return g_copy(zz * NY + y, h, gy_send, ypeer)

    def a_x(plane, h):
        return a_copy(plane, h, ax_send, xpeer)

    def g_c(plane, h):
        return g_copy(plane, h, gc_send, cpeer)

    def a_wait(plane, part, h):
        slot = a_slot(plane, part, h)
        remote(slot, slot, ax_send, a_recv.at[plane * 2 + part, h], xpeer).wait_recv()

    def g_wait(plane, part, h):
        slot = g_slot(plane, part, h)
        remote(slot, slot, gc_send, g_recv.at[plane * 2 + part, h], cpeer).wait_recv()

    own_a = pltpu.make_async_copy(
        act_hbm.at[0], actg.at[s, pl.ds(pl.multiple_of(x * cb, cb), cb), :], in_sem.at[0]
    )
    own_g = pltpu.make_async_copy(
        grad_hbm.at[0], gradg.at[s, :, pl.ds(pl.multiple_of(c * half, half), half)], in_sem.at[1]
    )
    own_a.start()
    own_g.start()
    barrier = pltpu.get_barrier_semaphore()

    def signal(device):
        pl.semaphore_signal(barrier, inc=1, device_id=device, device_id_type=MESH)

    for way in (-1, 1):
        @pl.when(inside(z + way))
        def _():
            signal(zpeer(way))
    for peer in (ypeer, cpeer, xpeer):
        signal(peer)
    w_copy = pltpu.make_async_copy(w_hbm, w, w_sem.at[0])
    w_copy.start()

    def wf_copy(i):
        a, b, k = i // 9, i // 3 % 3, i % 3
        return pltpu.make_async_copy(
            w_hbm.at[a, b, k], wf.at[a, b, :, k * chans : (k + 1) * chans], w_sem.at[1]
        )

    for i in range(27):
        wf_copy(i).start()

    own_a.wait()
    own_g.wait()
    pl.semaphore_wait(barrier, 3 + (z + NZ - 1) // NZ + (2 * NZ - 2 - z) // NZ)

    for h in range(H):
        for way in (-1, 1):
            @pl.when(inside(z + way))
            def _():
                a_z(z, way, h).start()
        a_y(z, h).start()
        a_x(s, h).start()
        for way in (-1, 1):
            @pl.when(inside(z + way))
            def _():
                g_z(z, way, h).start()
        g_y(z, h).start()
        g_c(s, h).start()

    @pl.loop(0, S)
    def _(j):
        wide[j, 0:W, :] = jnp.zeros((W, 3 * chans), bf16)
        wide[j, W + cells : 2 * W + cells, :] = jnp.zeros((W, 3 * chans), bf16)

    for j in range(3):
        gwide[j, 0:W, :] = jnp.zeros((W, 3 * filters), bf16)
        gwide[j, W + cells : 2 * W + cells, :] = jnp.zeros((W, 3 * filters), bf16)

    @pl.loop(0, 27)
    def _(i):
        acc[i // 9, i // 3 % 3, i % 3] = jnp.zeros((filters, chans), f32)

    def from_z(d, wait, part, along):
        for way in (-1, 1):
            zz = z + way * d

            @pl.when(inside(zz))
            def _():
                for h in range(H):
                    wait(zz * NY + y, part, h)

                    @pl.when(inside(z - way))
                    def _():
                        along(zz, -way, h).start()

    def a_hand(zz):
        @pl.when(inside(zz))
        def _():
            for h in range(H):
                a_y(zz, h).start()
                a_x(zz * NY + y, h).start()

    def g_hand(zz):
        @pl.when(inside(zz))
        def _():
            for h in range(H):
                g_y(zz, h).start()
                g_c(zz * NY + y, h).start()

    def a_from_z(d):
        from_z(d, a_wait, x, a_z)

    def g_from_z(d):
        from_z(d, g_wait, c, g_z)

    def at_two(hand):
        hand(z + 2)
        hand(z - 2)

    def at_three(hand):
        hand(z + 3)
        hand(z - 3)

    def a_from_y(zz):
        for h in range(H):
            a_wait(zz * NY + oy, x, h)
            a_x(zz * NY + oy, h).start()

    def g_from_y(zz):
        for h in range(H):
            g_wait(zz * NY + oy, c, h)
            g_c(zz * NY + oy, h).start()

    def a_rest(plane):
        for h in range(H):
            a_wait(plane, 1 - x, h)

    def g_rest(plane):
        for h in range(H):
            g_wait(plane, 1 - c, h)

    def window(plane, b):
        return wide[plane, b * W : b * W + cells, :]

    def prepare(plane):
        def store(k, value):
            wide[plane, W : W + cells, k * chans : (k + 1) * chans] = value

        shifted_copies(actg[plane].astype(f32).T, store)

    scale = 1.0 / math.sqrt(S * cells)

    def add(a, b, value):
        for k in range(3):
            acc[a, b, k] += value[:, k * chans : (k + 1) * chans] * scale

    def block(wp, gp):
        grad = gradg[gp]
        for b in range(3):
            add(wp - gp + 1, b, jnp.dot(grad, window(wp, b), preferred_element_type=f32))

    def in_pair(wp, zz):
        grads = gradg[pl.ds(zz * NY, NY)].reshape(NY * filters, cells)
        at = wp - zz * NY
        for b in range(3):
            value = jnp.dot(grads, window(wp, b), preferred_element_type=f32)
            add(at + 1, b, value[:filters])
            add(at, b, value[filters:])

    def backward(j, plane):
        def store(k, value):
            at = (2 - k) * filters
            gwide[j, W : W + cells, at : at + filters] = value

        shifted_copies(gradg[plane].astype(f32).T, store)
        a = s + 1 - plane
        total = None
        for b in range(3):
            rows = slice((2 - b) * W, (2 - b) * W + cells)
            taps = w[a, b].reshape(3 * filters, chans)
            term = jnp.dot(gwide[j, rows, :], taps, preferred_element_type=f32)
            total = term if total is None else total + term
        bacc[...] = total if j == 0 else bacc[...] + total

    def forward(j, plane):
        a = plane - s + 1
        total = None
        for b in range(3):
            term = lax.dot_general(
                window(plane, b), wf[a, b], (((1,), (1,)), ((), ())), preferred_element_type=f32
            )
            total = term if total is None else total + term
        facc[...] = total if j == 0 else facc[...] + total

    p_rows = cb // parts

    def b_copy(i):
        return remote(
            bpart.at[pl.ds(pl.multiple_of((1 - x) * cb + i * p_rows, p_rows), p_rows), :],
            brecv.at[pl.ds(i * p_rows, p_rows), :], b_send.at[i], b_recv.at[i], xpeer,
        )

    f_copy = remote(
        fpart.at[:, pl.ds(pl.multiple_of((1 - c) * half, half), half)], frecv, f_send, f_recv, cpeer
    )
    side = 2 * y - 1
    end = (z == 0) | (z == NZ - 1)
    inner = jnp.where(z < NZ // 2, 1, -1)
    third = s + side
    near_z = jnp.where(end, z + inner, z - side)
    far_z = jnp.where(end, -1, z + side)
    late = jnp.logical_not(end) & (side != inner)
    inner = jnp.where(z < NZ // 2, 1, -1)

    def order(o):
        return pair_at(z, y, NZ, o)

    exists = (third >= 0) & (third < S)

    other = z * NY + oy
    w_copy.wait()
    g_rest(s)
    backward(0, s)
    a_from_y(z)
    a_from_z(1)
    a_hand(near_z)
    pltpu.make_async_copy(w_hbm, w, w_sem.at[1]).wait()
    a_rest(s)
    prepare(s)
    block(s, s)
    g_from_y(z)
    g_from_z(1)
    g_hand(near_z)
    a_hand(far_z)
    g_hand(far_z)
    forward(0, s)
    g_rest(other)
    backward(1, other)
    a_from_y(order(1))
    a_from_z(2)
    at_two(a_hand)
    block(s, other)
    a_rest(other)
    prepare(other)
    in_pair(other, z)
    g_from_y(order(1))
    g_from_z(2)
    at_two(g_hand)
    forward(1, other)

    @pl.loop(1, NZ)
    def _(o):
        zz = order(o)
        nxt = order(jnp.minimum(o + 1, NZ - 1))
        mine, theirs = zz * NY + y, zz * NY + oy
        a_rest(mine)
        prepare(mine)
        g_rest(mine)
        g_rest(theirs)
        in_pair(mine, zz)

        @pl.when(o == 1)
        def _():
            a_from_y(nxt)


        @pl.when(o == 2)
        def _():
            a_from_y(nxt)
            b_copy(1).start()


        @pl.when(o == 3)
        def _():
            b_copy(3).start()

        a_rest(theirs)
        prepare(theirs)
        pl.when(o < NZ - 1)(lambda: in_pair(theirs, zz))

        @pl.when(o == 1)
        def _():
            a_from_z(3)
            at_three(a_hand)
            g_from_y(nxt)


        @pl.when(o == 2)
        def _():
            g_from_y(nxt)

        low = jnp.where(zz > z, zz * NY - 1, zz * NY + NY - 1)
        pl.when(o < NZ - 1)(lambda: block(low, low + 1))
        pl.when(o < NZ - 1)(lambda: block(low + 1, low))

        @pl.when(o == 1)
        def _():
            g_from_z(3)
            at_three(g_hand)
            pl.when(exists)(lambda: backward(2, third))
            bpart[...] = bacc[...].T
            b_copy(0).start()


        @pl.when(o == 2)
        def _():
            b_copy(2).start()


        @pl.when(o == 1)
        def _():
            pl.when(exists)(lambda: forward(2, third))
            fpart[...] = facc[...].T
            f_copy.start()


    f_copy.wait()
    out_ref[0] = (fpart[:, pl.ds(pl.multiple_of(c * half, half), half)] + frecv[...]).astype(bf16)
    for i in range(parts):
        b_copy(i).wait()
    ig_ref[0] = (bpart[pl.ds(pl.multiple_of(x * cb, cb), cb), :] + brecv[...]).astype(bf16)

    def sent(n, a_send, g_send, a_peer, g_peer):
        a_all = actg.at[0:n, 0:cb, :]
        g_all = gradg.at[0:n, :, 0:half]
        remote(a_all, a_all, a_send, a_recv.at[0, 0], a_peer).wait_send()
        remote(g_all, g_all, g_send, g_recv.at[0, 0], g_peer).wait_send()

    sent(NZ, ay_send, gy_send, ypeer, ypeer)
    sent(S, ax_send, gc_send, xpeer, cpeer)
    pl.when(end)(lambda: sent(1, az_send, gz_send, ypeer, ypeer))
    pl.when(jnp.logical_not(end))(lambda: sent(NZ + 1, az_send, gz_send, ypeer, ypeer))


def near_body(activation, weights, out_grad):
    S = lax.axis_size("space")
    NY, H, parts = 2, 1, 4
    NZ = S // NY
    cb, cells = activation.shape[1:]
    filters, half = out_grad.shape[1:]
    chans = 2 * cb
    bf16, f32 = jnp.bfloat16, jnp.float32
    dma = pltpu.SemaphoreType.DMA
    vmem = pl.BlockSpec(memory_space=pltpu.VMEM)
    hbm = pl.BlockSpec(memory_space=pltpu.HBM)
    shapes = ((out_grad.shape, bf16), (activation.shape, bf16), (weights.shape, f32))
    kept = (((S, filters, cells), bf16), ((S, cells + 2 * W, 3 * chans), bf16))
    found = pl.pallas_call(
        near_kernel,
        out_shape=tuple(pltpu.VMEM(*shape) for shape in shapes + kept),
        in_specs=[hbm, hbm, hbm],
        out_specs=(vmem,) * 5,
        scratch_shapes=[
            pltpu.VMEM((S, chans, cells), bf16),
            pltpu.VMEM((3, cells + 2 * W, 3 * filters), bf16),
            pltpu.VMEM(weights.shape, bf16),
            pltpu.VMEM((3, 3, filters, 3 * chans), bf16),
            pltpu.VMEM((cells, filters), f32),
            pltpu.VMEM((cells, chans), f32),
            pltpu.VMEM((filters, cells), f32),
            pltpu.VMEM((chans, cells), f32),
            pltpu.VMEM((filters, half), f32),
            pltpu.VMEM((cb, cells), f32),
            dma((2,)), dma((2,)),
            dma, dma, dma, dma, dma, dma,
            dma((S * 2, H)), dma((S * 2, H)),
            dma, dma, dma((parts,)), dma((parts,)),
        ],
        compiler_params=pltpu.CompilerParams(
            collective_id=1, has_side_effects=True, vmem_limit_bytes=45 * 1024 * 1024
        ),
    )(activation, weights, out_grad)
    return pl.pallas_call(
        last_kernel,
        out_shape=tuple(jax.ShapeDtypeStruct(*shape) for shape in shapes),
        in_specs=[vmem] * 5,
        out_specs=(hbm, hbm, hbm),
        scratch_shapes=[pltpu.VMEM(weights.shape, f32), dma, dma, dma],
        compiler_params=pltpu.CompilerParams(vmem_limit_bytes=16 * 1024 * 1024),
    )(*found)


def solution(mesh):
    placed = (
        P("space", ("chan", "filt"), None),
        P(None, None, None, "filt", "chan"),
        P("space", "filt", "chan"),
    )
    near = mesh.shape["space"] == 8 and mesh.shape["filt"] == 2 and mesh.shape["chan"] == 2
    return jax.shard_map(
        near_body if near else body,
        mesh=mesh,
        in_specs=placed,
        out_specs=(
            P("space", "filt", "chan"),
            P("space", ("chan", "filt"), None),
            P(None, None, None, "filt", "chan"),
        ),
        check_vma=False,
    )
```

```python
import functools
import math

import jax
import jax.numpy as jnp
from jax import lax
from jax.experimental import pallas as pl
from jax.experimental.pallas import tpu as pltpu
from jax.sharding import PartitionSpec as P

W = 16
MESH = pl.DeviceIdType.MESH


def shifted_copies(t, store):
    cells = t.shape[0]
    column = lax.broadcasted_iota(jnp.int32, t.shape, 0) % W
    store(0, jnp.where(column >= 1, pltpu.roll(t, 1, 0), 0.0).astype(jnp.bfloat16))
    store(1, t.astype(jnp.bfloat16))
    store(2, jnp.where(column <= W - 2, pltpu.roll(t, cells - 1, 0), 0.0).astype(jnp.bfloat16))


def kernel(
    sizes, act_ref, w_hbm, grad_ref, out_ref, ig_ref, acc,
    actg, gradg, wide, gwide, w, wf, facc, bacc, fpart, bpart, frecv, brecv,
    w_sem, wf_sem, az_send, ay_send, ax_send, gz_send, gy_send, gc_send,
    a_recv, g_recv, f_send, f_recv, b_send, b_recv,
):
    S, NX, NZ, NY = sizes
    cb, cells = act_ref.shape[1:]
    filters, half = grad_ref.shape[1:]
    chans = NX * cb
    s = lax.axis_index("space")
    c = lax.axis_index("chan")
    x = lax.axis_index("filt")
    z, y = s // NY, s % NY
    oy = 1 - y
    f32, bf16 = jnp.float32, jnp.bfloat16

    def remote(src, dst, send, recv, device):
        return pltpu.make_async_remote_copy(
            src_ref=src, dst_ref=dst, send_sem=send, recv_sem=recv,
            device_id=device, device_id_type=MESH,
        )

    def signal(device):
        pl.semaphore_signal(barrier, inc=1, device_id=device, device_id_type=MESH)

    def a_slot(plane, part):
        return actg.at[plane, pl.ds(pl.multiple_of(part * cb, cb), cb), :]

    def g_slot(plane, part):
        return gradg.at[plane + 1, :, pl.ds(pl.multiple_of(part * half, half), half)]

    ypeer = {"space": z * NY + oy}
    xpeers = [{"filt": (x + e) % NX} for e in range(1, NX)]
    cpeer = {"chan": 1 - c}

    def a_copy(plane, send, device):
        slot = a_slot(plane, x)
        return remote(slot, slot, send, a_recv.at[plane * NX + x], device)

    def g_copy(plane, send, device):
        slot = g_slot(plane, c)
        return remote(slot, slot, send, g_recv.at[plane * 2 + c], device)

    def a_wait(plane, part):
        slot = a_slot(plane, part)
        remote(slot, slot, ay_send.at[0], a_recv.at[plane * NX + part], ypeer).wait_recv()

    def g_wait(plane, part):
        slot = g_slot(plane, part)
        remote(slot, slot, gy_send.at[0], g_recv.at[plane * 2 + part], ypeer).wait_recv()

    def a_z(zz, way):
        to = {"space": (z + way) * NY + y}
        return a_copy(zz * NY + y, az_send.at[(way + 1) // 2 * NZ + zz], to)

    def g_z(zz, way):
        to = {"space": (z + way) * NY + y}
        return g_copy(zz * NY + y, gz_send.at[(way + 1) // 2 * NZ + zz], to)

    def a_y(zz):
        return a_copy(zz * NY + y, ay_send.at[zz], ypeer)

    def g_y(zz):
        return g_copy(zz * NY + y, gy_send.at[zz], ypeer)

    def a_x(plane, e):
        return a_copy(plane, ax_send.at[plane * (NX - 1) + e - 1], xpeers[e - 1])

    def g_c(plane):
        return g_copy(plane, gc_send.at[plane], cpeer)

    def start_x(plane):
        for e in range(1, NX):
            a_x(plane, e).start()

    def inside(zz):
        return (zz >= 0) & (zz < NZ)

    def at_distance(d, run):
        @pl.when(inside(z - d))
        def _():
            run(z - d, -1)

        @pl.when((d > 0) & inside(z + d))
        def _():
            run(z + d, 1)

    actg[s, pl.ds(pl.multiple_of(x * cb, cb), cb), :] = act_ref[0]
    gradg[s + 1, :, pl.ds(pl.multiple_of(c * half, half), half)] = grad_ref[0]
    barrier = pltpu.get_barrier_semaphore()
    for way in (-1, 1):
        @pl.when(inside(z + way))
        def _():
            signal({"space": (z + way) * NY + y})
    for peer in [ypeer, cpeer] + xpeers:
        signal(peer)
    beside = (z + NZ - 1) // NZ + (2 * NZ - 2 - z) // NZ
    pl.semaphore_wait(barrier, NX + 1 + beside)

    for way in (-1, 1):
        @pl.when(inside(z + way))
        def _():
            a_z(z, way).start()
    a_y(z).start()
    start_x(s)
    for way in (-1, 1):
        @pl.when(inside(z + way))
        def _():
            g_z(z, way).start()
    g_y(z).start()
    g_c(s).start()
    w_copy = pltpu.make_async_copy(w_hbm, w, w_sem)
    w_copy.start()

    def wf_copy(i):
        a, b, k = i // 9, i // 3 % 3, i % 3
        return pltpu.make_async_copy(
            w_hbm.at[a, b, k], wf.at[a, b, :, k * chans : (k + 1) * chans], wf_sem.at[i]
        )

    for i in range(27):
        wf_copy(i).start()

    for end in (0, S + 1):
        gradg[end] = jnp.zeros((filters, cells), bf16)
        wide[end] = jnp.zeros(wide.shape[1:], bf16)

    @pl.loop(1, S + 1)
    def _(j):
        wide[j, 0:W, :] = jnp.zeros((W, 3 * chans), bf16)
        wide[j, W + cells : 2 * W + cells, :] = jnp.zeros((W, 3 * chans), bf16)

    for j in range(3):
        gwide[j, 0:W, :] = jnp.zeros((W, gwide.shape[2]), bf16)
        gwide[j, W + cells : 2 * W + cells, :] = jnp.zeros((W, gwide.shape[2]), bf16)

    @pl.loop(0, 27)
    def _(i):
        acc[i // 9, i // 3 % 3, i % 3] = jnp.zeros((filters, chans), f32)

    facc[...] = jnp.zeros_like(facc)
    bacc[...] = jnp.zeros_like(bacc)
    w_copy.wait()
    for i in range(27):
        wf_copy(i).wait()

    lanes = gwide.shape[2] // 3

    def b_copy(e):
        to = (x + e) % NX
        return remote(
            bpart.at[pl.ds(pl.multiple_of(to * cb, cb), cb), :],
            brecv.at[e - 1], b_send.at[e - 1], b_recv.at[e - 1], xpeers[e - 1],
        )

    f_copy = remote(
        fpart.at[:, pl.ds(pl.multiple_of((1 - c) * half, half), half)], frecv, f_send, f_recv, cpeer
    )

    def window(plane, b):
        return wide[plane + 1, pl.ds(pl.multiple_of(b * W, W), cells), :]

    def backward():
        @pl.loop(0, 3)
        def _(j):
            def store(k, value):
                at = (2 - k) * lanes
                gwide[j, W : W + cells, at : at + filters] = value

            shifted_copies(gradg[s + j].astype(f32).T, store)

        @pl.loop(0, 3)
        def _(a):
            total = None
            for b in range(3):
                rows = slice((2 - b) * W, (2 - b) * W + cells)
                if lanes == filters:
                    taps = w[a, b].reshape(3 * filters, chans)
                    terms = [jnp.dot(gwide[2 - a, rows, :], taps, preferred_element_type=f32)]
                else:
                    terms = [
                        jnp.dot(
                            gwide[2 - a, rows, k * lanes : k * lanes + filters],
                            w[a, b, k], preferred_element_type=f32,
                        )
                        for k in range(3)
                    ]
                for term in terms:
                    total = term if total is None else total + term
            bacc[...] += total

        bpart[...] = bacc[...].T

    def send_backward():
        for e in range(1, NX):
            b_copy(e).start()

    def forward():
        @pl.loop(0, 3)
        def _(a):
            total = None
            for b in range(3):
                term = lax.dot_general(
                    window(s + a - 1, b), wf[a, b], (((1,), (1,)), ((), ())), preferred_element_type=f32
                )
                total = term if total is None else total + term
            facc[...] += total

        fpart[...] = facc[...].T
        f_copy.start()

    def prepare(zz):
        @pl.loop(0, NY)
        def _(i):
            plane = zz * NY + i
            for e in range(1, NX):
                a_wait(plane, (x + e) % NX)

            def store(k, value):
                wide[plane + 1, W : W + cells, k * chans : (k + 1) * chans] = value

            shifted_copies(actg[plane].astype(f32).T, store)

    scale = 1.0 / math.sqrt(S * cells)

    def add(a, b, value):
        for k in range(3):
            acc[a, b, k] += value[:, k * chans : (k + 1) * chans] * scale

    def in_pair(zz):
        @pl.loop(0, 3)
        def _(b):
            j = zz * NY
            grads = gradg[pl.ds(j + 1, 2)].reshape(2 * filters, cells)
            low = jnp.dot(grads, window(j, b), preferred_element_type=f32)
            high = jnp.dot(grads, window(j + 1, b), preferred_element_type=f32)
            add(0, b, low[filters:])
            add(1, b, low[:filters] + high[filters:])
            add(2, b, high[:filters])

    def across_pairs(zz):
        @pl.loop(0, 3)
        def _(b):
            j = zz * NY + 1
            add(0, b, jnp.dot(gradg[j + 2], window(j, b), preferred_element_type=f32))
            add(2, b, jnp.dot(gradg[j + 1], window(j + 1, b), preferred_element_type=f32))

    def filter_grad(zz, way):
        prepare(zz)
        in_pair(zz)

        @pl.when(zz != z)
        def _():
            across_pairs(zz + (-1 - way) // 2)

    def relay(zz, way, wait, along, across, last):
        plane = zz * NY + y
        wait(plane)

        @pl.when(inside(z - way))
        def _():
            along(zz, -way).start()

        across(zz).start()
        last(plane)

    def pass_on(zz, wait, last):
        plane = zz * NY + oy
        wait(plane)
        last(plane)

    def a_own(plane):
        a_wait(plane, x)

    def g_own(plane):
        g_wait(plane, c)

    def start_c(plane):
        g_c(plane).start()

    def core_halves(zz, way):
        for n in range(NY):
            g_wait(zz * NY + n, 1 - c)

    @pl.loop(1, NZ + 2)
    def _(d):
        at_distance(d - 1, lambda zz, way: pass_on(zz, a_own, start_x))
        at_distance(d, lambda zz, way: relay(zz, way, a_own, a_z, a_y, start_x))
        at_distance(d - 1, lambda zz, way: pass_on(zz, g_own, start_c))
        at_distance(d, lambda zz, way: relay(zz, way, g_own, g_z, g_y, start_c))
        at_distance(d - 1, core_halves)

        @pl.when(d == 2)
        def _():
            backward()

        @pl.when(d == 4)
        def _():
            send_backward()
            forward()

        @pl.when(d != 2)
        def _():
            at_distance(jnp.maximum(d - 2, 0), filter_grad)

    f_copy.wait()
    out_ref[0] = (fpart[:, pl.ds(pl.multiple_of(c * half, half), half)] + frecv[...]).astype(bf16)
    own = bpart[pl.ds(pl.multiple_of(x * cb, cb), cb), :]
    for e in range(1, NX):
        b_copy(e).wait()
        own = own + brecv[e - 1]
    ig_ref[0] = own.astype(bf16)

    @pl.loop(0, NZ)
    def _(zz):
        for way in (-1, 1):
            @pl.when(inside(z + way) & ((z - zz) * way >= 0))
            def _():
                a_z(zz, way).wait_send()
                g_z(zz, way).wait_send()
        a_y(zz).wait_send()
        g_y(zz).wait_send()

    @pl.loop(0, S)
    def _(plane):
        for e in range(1, NX):
            a_x(plane, e).wait_send()
        g_c(plane).wait_send()


def body(activation, weights, out_grad):
    S = lax.axis_size("space")
    NX = lax.axis_size("filt")
    NY = 2
    NZ = S // NY
    cb, cells = activation.shape[1:]
    filters, half = out_grad.shape[1:]
    chans = NX * cb
    bf16, f32 = jnp.bfloat16, jnp.float32
    dma = pltpu.SemaphoreType.DMA
    vmem = pl.BlockSpec(memory_space=pltpu.VMEM)
    hbm = pl.BlockSpec(memory_space=pl.ANY)
    shapes = ((out_grad.shape, bf16), (activation.shape, bf16), (weights.shape, f32))
    results = pl.pallas_call(
        functools.partial(kernel, (S, NX, NZ, NY)),
        out_shape=tuple(pltpu.VMEM(*shape) for shape in shapes),
        in_specs=[vmem, hbm, vmem],
        out_specs=(vmem, vmem, vmem),
        scratch_shapes=[
            pltpu.VMEM((S, chans, cells), bf16),
            pltpu.VMEM((S + 2, filters, cells), bf16),
            pltpu.VMEM((S + 2, cells + 2 * W, 3 * chans), bf16),
            pltpu.VMEM((3, cells + 2 * W, 3 * pl.cdiv(filters, 128) * 128), bf16),
            pltpu.VMEM(weights.shape, bf16),
            pltpu.VMEM((3, 3, filters, 3 * chans), bf16),
            pltpu.VMEM((cells, filters), f32),
            pltpu.VMEM((cells, chans), f32),
            pltpu.VMEM((filters, cells), f32),
            pltpu.VMEM((chans, cells), f32),
            pltpu.VMEM((filters, half), f32),
            pltpu.VMEM((NX - 1, cb, cells), f32),
            dma, dma((27,)),
            dma((2 * NZ,)), dma((NZ,)), dma((S * (NX - 1),)),
            dma((2 * NZ,)), dma((NZ,)), dma((S,)),
            dma((S * NX,)), dma((S * 2,)),
            dma, dma, dma((NX - 1,)), dma((NX - 1,)),
        ],
        compiler_params=pltpu.CompilerParams(
            collective_id=0, has_side_effects=True, vmem_limit_bytes=50 * 1024 * 1024
        ),
    )(activation, weights, out_grad)
    return results


def pair_at(z, y, NZ, o):
    side = 2 * y - 1
    out = jnp.where(z == 0, o, NZ - 1 - o)
    last = jnp.where(z == 1, NZ - 1, 0)
    mid = jnp.where(o == 1, z + side, jnp.where(o == 2, z - side, jnp.where(o == 3, last, z)))
    return jnp.where((z == 0) | (z == NZ - 1), out, mid)


def last_kernel(
    out_ref, ig_ref, acc, gradg, wide, out_hbm, ig_hbm, kg_hbm, stage, out_sem, ig_sem, kg_sem
):
    NY, NZ = 2, 4
    S, filters, cells = gradg.shape
    chans = acc.shape[-1]
    s = lax.axis_index("space")
    z, y = s // NY, s % NY
    oy = 1 - y
    f32 = jnp.float32
    out_copy = pltpu.make_async_copy(out_ref, out_hbm, out_sem)
    ig_copy = pltpu.make_async_copy(ig_ref, ig_hbm, ig_sem)
    out_copy.start()
    ig_copy.start()
    zz = pair_at(z, y, NZ, NZ - 1)
    low = jnp.where(zz > z, zz * NY - 1, zz * NY + NY - 1)
    scale = 1.0 / math.sqrt(S * cells)

    def part(value, k):
        return value[:, k * chans : (k + 1) * chans] * scale

    for b in range(3):
        def window(plane):
            return wide[plane, b * W : b * W + cells, :]

        before = jnp.dot(gradg[low + 1], window(low), preferred_element_type=f32)
        after = jnp.dot(gradg[low], window(low + 1), preferred_element_type=f32)
        for k in range(3):
            stage[0, b, k] = acc[0, b, k] + part(before, k)
            stage[1, b, k] = acc[1, b, k]
            stage[2, b, k] = acc[2, b, k] + part(after, k)
        grads = gradg[pl.ds(zz * NY, NY)].reshape(NY * filters, cells)
        value = jnp.dot(grads, window(zz * NY + oy), preferred_element_type=f32)
        for k in range(3):
            stage[oy + 1, b, k] += part(value[:filters], k)
            stage[oy, b, k] += part(value[filters:], k)
        for a in range(3):
            pltpu.make_async_copy(stage.at[a, b], kg_hbm.at[a, b], kg_sem).start()
    out_copy.wait()
    ig_copy.wait()
    pltpu.make_async_copy(stage, kg_hbm, kg_sem).wait()


def near_kernel(
    act_hbm, w_hbm, grad_hbm, out_ref, ig_ref, acc, gradg, wide,
    actg, gwide, w, wf, facc, bacc, fpart, bpart, frecv, brecv,
    in_sem, w_sem, az_send, ay_send, ax_send, gz_send, gy_send, gc_send,
    a_recv, g_recv, f_send, f_recv, b_send, b_recv, p_send,
):
    NY, NZ, H, parts = 2, 4, 1, 2
    S = NY * NZ
    cb, cells = act_hbm.shape[1:]
    filters, half = grad_hbm.shape[1:]
    chans = 2 * cb
    a_rows, g_rows = cb // H, filters // H
    s = lax.axis_index("space")
    c = lax.axis_index("chan")
    x = lax.axis_index("filt")
    z, y = s // NY, s % NY
    oy = 1 - y
    end = (z == 0) | (z == NZ - 1)
    inner = jnp.where(z < NZ // 2, 1, -1)
    f32, bf16 = jnp.float32, jnp.bfloat16
    ypeer = {"space": z * NY + oy}
    xpeer = {"filt": 1 - x}
    cpeer = {"chan": 1 - c}

    def zpeer(way):
        return {"space": (z + way) * NY + y}

    def inside(zz):
        return (zz >= 0) & (zz < NZ)

    def remote(src, dst, send, recv, device):
        return pltpu.make_async_remote_copy(
            src_ref=src, dst_ref=dst, send_sem=send, recv_sem=recv,
            device_id=device, device_id_type=MESH,
        )

    def a_slot(plane, part, h):
        return actg.at[plane, pl.ds(pl.multiple_of(part * cb + h * a_rows, a_rows), a_rows), :]

    def g_slot(plane, part, h):
        return gradg.at[plane, pl.ds(h * g_rows, g_rows), pl.ds(pl.multiple_of(part * half, half), half)]

    def a_copy(plane, h, send, device):
        slot = a_slot(plane, x, h)
        return remote(slot, slot, send, a_recv.at[plane * 2 + x, h], device)

    def g_copy(plane, h, send, device):
        slot = g_slot(plane, c, h)
        return remote(slot, slot, send, g_recv.at[plane * 2 + c, h], device)

    def a_z(zz, way, h):
        return a_copy(zz * NY + y, h, az_send, zpeer(way))

    def g_z(zz, way, h):
        return g_copy(zz * NY + y, h, gz_send, zpeer(way))

    def a_y(zz, h):
        return a_copy(zz * NY + y, h, ay_send, ypeer)

    def g_y(zz, h):
        return g_copy(zz * NY + y, h, gy_send, ypeer)

    def a_x(plane, h):
        return a_copy(plane, h, ax_send, xpeer)

    by_z = jnp.where(end, z + 2 * inner, z - inner)
    pass_on = jnp.where(end, z, z + inner)

    def start_x(plane, h):
        @pl.when(plane != by_z * NY + y)
        def _():
            a_x(plane, h).start()

    def p_copy(plane, h):
        slot = a_slot(plane, 1 - x, h)
        return remote(
            slot, slot, p_send.at[h], a_recv.at[plane * 2 + 1 - x, h],
            zpeer(jnp.where(end, inner, -inner)),
        )

    def g_c(plane, h):
        return g_copy(plane, h, gc_send, cpeer)

    def a_wait(plane, part, h):
        slot = a_slot(plane, part, h)
        remote(slot, slot, ax_send, a_recv.at[plane * 2 + part, h], xpeer).wait_recv()

    def g_wait(plane, part, h):
        slot = g_slot(plane, part, h)
        remote(slot, slot, gc_send, g_recv.at[plane * 2 + part, h], cpeer).wait_recv()

    own_a = pltpu.make_async_copy(
        act_hbm.at[0], actg.at[s, pl.ds(pl.multiple_of(x * cb, cb), cb), :], in_sem.at[0]
    )
    own_g = pltpu.make_async_copy(
        grad_hbm.at[0], gradg.at[s, :, pl.ds(pl.multiple_of(c * half, half), half)], in_sem.at[1]
    )
    own_a.start()
    own_g.start()
    barrier = pltpu.get_barrier_semaphore()

    def signal(device):
        pl.semaphore_signal(barrier, inc=1, device_id=device, device_id_type=MESH)

    for way in (-1, 1):
        @pl.when(inside(z + way))
        def _():
            signal(zpeer(way))
    for peer in (ypeer, cpeer, xpeer):
        signal(peer)
    w_copy = pltpu.make_async_copy(w_hbm, w, w_sem.at[0])
    w_copy.start()

    def wf_copy(i):
        a, b, k = i // 9, i // 3 % 3, i % 3
        return pltpu.make_async_copy(
            w_hbm.at[a, b, k], wf.at[a, b, :, k * chans : (k + 1) * chans], w_sem.at[1]
        )

    for i in range(27):
        wf_copy(i).start()

    own_a.wait()
    own_g.wait()
    pl.semaphore_wait(barrier, 3 + (z + NZ - 1) // NZ + (2 * NZ - 2 - z) // NZ)

    for h in range(H):
        for way in (-1, 1):
            @pl.when(inside(z + way))
            def _():
                a_z(z, way, h).start()
        a_y(z, h).start()
        a_x(s, h).start()
        for way in (-1, 1):
            @pl.when(inside(z + way))
            def _():
                g_z(z, way, h).start()
        g_y(z, h).start()
        g_c(s, h).start()

    @pl.loop(0, S)
    def _(j):
        wide[j, 0:W, :] = jnp.zeros((W, 3 * chans), bf16)
        wide[j, W + cells : 2 * W + cells, :] = jnp.zeros((W, 3 * chans), bf16)

    for j in range(3):
        gwide[j, 0:W, :] = jnp.zeros((W, 3 * filters), bf16)
        gwide[j, W + cells : 2 * W + cells, :] = jnp.zeros((W, 3 * filters), bf16)

    @pl.loop(0, 27)
    def _(i):
        acc[i // 9, i // 3 % 3, i % 3] = jnp.zeros((filters, chans), f32)

    def from_z(d, wait, part, along):
        for way in (-1, 1):
            zz = z + way * d

            @pl.when(inside(zz))
            def _():
                for h in range(H):
                    wait(zz * NY + y, part, h)

                    @pl.when(inside(z - way))
                    def _():
                        along(zz, -way, h).start()

    def a_hand(zz):
        @pl.when(inside(zz))
        def _():
            for h in range(H):
                a_y(zz, h).start()
                start_x(zz * NY + y, h)

    def g_hand(zz):
        @pl.when(inside(zz))
        def _():
            for h in range(H):
                g_y(zz, h).start()
                g_c(zz * NY + y, h).start()

    def a_from_z(d):
        from_z(d, a_wait, x, a_z)

    def g_from_z(d):
        from_z(d, g_wait, c, g_z)

    def at_two(hand):
        hand(z + 2)
        hand(z - 2)

    def at_three(hand):
        hand(z + 3)
        hand(z - 3)

    def a_from_y(zz):
        for h in range(H):
            a_wait(zz * NY + oy, x, h)
            a_x(zz * NY + oy, h).start()

    def g_from_y(zz):
        for h in range(H):
            g_wait(zz * NY + oy, c, h)
            g_c(zz * NY + oy, h).start()

    def a_rest(plane):
        for h in range(H):
            a_wait(plane, 1 - x, h)

    def a_rest_on(plane, go):
        for h in range(H):
            a_wait(plane, 1 - x, h)

            @pl.when(go)
            def _():
                p_copy(plane, h).start()

    def g_rest(plane):
        for h in range(H):
            g_wait(plane, 1 - c, h)

    def window(plane, b):
        return wide[plane, b * W : b * W + cells, :]

    def prepare(plane):
        def store(k, value):
            wide[plane, W : W + cells, k * chans : (k + 1) * chans] = value

        shifted_copies(actg[plane].astype(f32).T, store)

    scale = 1.0 / math.sqrt(S * cells)

    def add(a, b, value):
        for k in range(3):
            acc[a, b, k] += value[:, k * chans : (k + 1) * chans] * scale

    def block(wp, gp):
        grad = gradg[gp]
        for b in range(3):
            add(wp - gp + 1, b, jnp.dot(grad, window(wp, b), preferred_element_type=f32))

    def in_pair(wp, zz):
        grads = gradg[pl.ds(zz * NY, NY)].reshape(NY * filters, cells)
        at = wp - zz * NY
        for b in range(3):
            value = jnp.dot(grads, window(wp, b), preferred_element_type=f32)
            add(at + 1, b, value[:filters])
            add(at, b, value[filters:])

    def backward(j, plane):
        def store(k, value):
            at = (2 - k) * filters
            gwide[j, W : W + cells, at : at + filters] = value

        shifted_copies(gradg[plane].astype(f32).T, store)
        a = s + 1 - plane
        total = None
        for b in range(3):
            rows = slice((2 - b) * W, (2 - b) * W + cells)
            taps = w[a, b].reshape(3 * filters, chans)
            term = jnp.dot(gwide[j, rows, :], taps, preferred_element_type=f32)
            total = term if total is None else total + term
        bacc[...] = total if j == 0 else bacc[...] + total

    def forward(j, plane):
        a = plane - s + 1
        total = None
        for b in range(3):
            term = lax.dot_general(
                window(plane, b), wf[a, b], (((1,), (1,)), ((), ())), preferred_element_type=f32
            )
            total = term if total is None else total + term
        facc[...] = total if j == 0 else facc[...] + total

    p_rows = cb // parts

    def b_copy(i):
        return remote(
            bpart.at[pl.ds(pl.multiple_of((1 - x) * cb + i * p_rows, p_rows), p_rows), :],
            brecv.at[pl.ds(i * p_rows, p_rows), :], b_send.at[i], b_recv.at[i], xpeer,
        )

    f_copy = remote(
        fpart.at[:, pl.ds(pl.multiple_of((1 - c) * half, half), half)], frecv, f_send, f_recv, cpeer
    )
    side = 2 * y - 1
    third = s + side
    near_z = jnp.where(end, z + inner, z - side)
    far_z = jnp.where(end, -1, z + side)

    def order(o):
        return pair_at(z, y, NZ, o)

    exists = (third >= 0) & (third < S)

    other = z * NY + oy
    w_copy.wait()
    g_rest(s)
    backward(0, s)
    a_from_y(z)
    a_from_z(1)
    a_hand(near_z)
    g_from_z(1)
    g_hand(near_z)
    a_hand(far_z)
    g_hand(far_z)
    g_from_y(z)
    a_rest_on(s, end)
    prepare(s)
    block(s, s)
    a_from_z(2)
    at_two(a_hand)
    a_from_y(order(1))
    g_rest(other)
    backward(1, other)
    a_rest(other)
    prepare(other)
    block(s, other)
    g_from_y(order(1))
    g_from_z(2)
    at_two(g_hand)
    a_from_z(3)
    at_three(a_hand)
    pltpu.make_async_copy(w_hbm, w, w_sem.at[1]).wait()
    forward(0, s)
    in_pair(other, z)
    forward(1, other)
    pl.when(jnp.logical_not(end))(lambda: a_rest_on(pass_on * NY + y, z >= 0))
    a_from_y(order(2))

    @pl.loop(1, NZ)
    def _(o):
        zz = order(o)
        mine, theirs = zz * NY + y, zz * NY + oy
        pl.when(end | (zz != pass_on))(lambda: a_rest(mine))
        prepare(mine)

        @pl.when(o == 2)
        def _():
            b_copy(1).start()

        g_rest(mine)
        g_rest(theirs)
        in_pair(mine, zz)

        @pl.when(o == 1)
        def _():
            pl.when(exists)(lambda: backward(2, third))
            bpart[...] = bacc[...].T

        a_rest(theirs)
        prepare(theirs)

        @pl.when(o == 1)
        def _():
            b_copy(0).start()
            g_from_y(order(2))

        pl.when(o < NZ - 1)(lambda: in_pair(theirs, zz))
        low = jnp.where(zz > z, zz * NY - 1, zz * NY + NY - 1)
        pl.when(o < NZ - 1)(lambda: block(low, low + 1))

        @pl.when(o == 1)
        def _():
            g_from_z(3)
            at_three(g_hand)


        @pl.when(o == 2)
        def _():
            g_from_y(order(3))

        pl.when(o < NZ - 1)(lambda: block(low + 1, low))

        @pl.when(o == 1)
        def _():
            a_from_y(order(3))
            pl.when(exists)(lambda: forward(2, third))
            fpart[...] = facc[...].T
            f_copy.start()


    f_copy.wait()
    out_ref[0] = (fpart[:, pl.ds(pl.multiple_of(c * half, half), half)] + frecv[...]).astype(bf16)
    for i in range(parts):
        b_copy(i).wait()
    ig_ref[0] = (bpart[pl.ds(pl.multiple_of(x * cb, cb), cb), :] + brecv[...]).astype(bf16)

    def sent(n, a_send, g_send, a_peer, g_peer):
        a_all = actg.at[0:n, 0:cb, :]
        g_all = gradg.at[0:n, :, 0:half]
        remote(a_all, a_all, a_send, a_recv.at[0, 0], a_peer).wait_send()
        remote(g_all, g_all, g_send, g_recv.at[0, 0], g_peer).wait_send()

    sent(NZ, ay_send, gy_send, ypeer, ypeer)
    x_all = actg.at[0 : S - 1, 0:cb, :]
    remote(x_all, x_all, ax_send, a_recv.at[0, 0], xpeer).wait_send()
    c_all = gradg.at[0:S, :, 0:half]
    remote(c_all, c_all, gc_send, g_recv.at[0, 0], cpeer).wait_send()
    for h in range(H):
        p_copy(pass_on * NY + y, h).wait_send()
    pl.when(end)(lambda: sent(1, az_send, gz_send, ypeer, ypeer))
    pl.when(jnp.logical_not(end))(lambda: sent(NZ + 1, az_send, gz_send, ypeer, ypeer))


def near_body(activation, weights, out_grad):
    S = lax.axis_size("space")
    NY, H, parts = 2, 1, 2
    NZ = S // NY
    cb, cells = activation.shape[1:]
    filters, half = out_grad.shape[1:]
    chans = 2 * cb
    bf16, f32 = jnp.bfloat16, jnp.float32
    dma = pltpu.SemaphoreType.DMA
    vmem = pl.BlockSpec(memory_space=pltpu.VMEM)
    hbm = pl.BlockSpec(memory_space=pltpu.HBM)
    shapes = ((out_grad.shape, bf16), (activation.shape, bf16), (weights.shape, f32))
    kept = (((S, filters, cells), bf16), ((S, cells + 2 * W, 3 * chans), bf16))
    found = pl.pallas_call(
        near_kernel,
        out_shape=tuple(pltpu.VMEM(*shape) for shape in shapes + kept),
        in_specs=[hbm, hbm, hbm],
        out_specs=(vmem,) * 5,
        scratch_shapes=[
            pltpu.VMEM((S, chans, cells), bf16),
            pltpu.VMEM((3, cells + 2 * W, 3 * filters), bf16),
            pltpu.VMEM(weights.shape, bf16),
            pltpu.VMEM((3, 3, filters, 3 * chans), bf16),
            pltpu.VMEM((cells, filters), f32),
            pltpu.VMEM((cells, chans), f32),
            pltpu.VMEM((filters, cells), f32),
            pltpu.VMEM((chans, cells), f32),
            pltpu.VMEM((filters, half), f32),
            pltpu.VMEM((cb, cells), f32),
            dma((2,)), dma((2,)),
            dma, dma, dma, dma, dma, dma,
            dma((S * 2, H)), dma((S * 2, H)),
            dma, dma, dma((parts,)), dma((parts,)), dma((H,)),
        ],
        compiler_params=pltpu.CompilerParams(
            collective_id=1, has_side_effects=True, vmem_limit_bytes=45 * 1024 * 1024
        ),
    )(activation, weights, out_grad)
    return pl.pallas_call(
        last_kernel,
        out_shape=tuple(jax.ShapeDtypeStruct(*shape) for shape in shapes),
        in_specs=[vmem] * 5,
        out_specs=(hbm, hbm, hbm),
        scratch_shapes=[pltpu.VMEM(weights.shape, f32), dma, dma, dma],
        compiler_params=pltpu.CompilerParams(vmem_limit_bytes=16 * 1024 * 1024),
    )(*found)


def solution(mesh):
    placed = (
        P("space", ("chan", "filt"), None),
        P(None, None, None, "filt", "chan"),
        P("space", "filt", "chan"),
    )
    near = mesh.shape["space"] == 8 and mesh.shape["filt"] == 2 and mesh.shape["chan"] == 2
    return jax.shard_map(
        near_body if near else body,
        mesh=mesh,
        in_specs=placed,
        out_specs=(
            P("space", "filt", "chan"),
            P("space", ("chan", "filt"), None),
            P(None, None, None, "filt", "chan"),
        ),
        check_vma=False,
    )
```

```python
import functools
import math

import jax
import jax.numpy as jnp
from jax import lax
from jax.experimental import pallas as pl
from jax.experimental.pallas import tpu as pltpu
from jax.sharding import PartitionSpec as P

W = 16
MESH = pl.DeviceIdType.MESH


def shifted_copies(t, store):
    cells = t.shape[0]
    column = lax.broadcasted_iota(jnp.int32, t.shape, 0) % W
    store(0, jnp.where(column >= 1, pltpu.roll(t, 1, 0), 0.0).astype(jnp.bfloat16))
    store(1, t.astype(jnp.bfloat16))
    store(2, jnp.where(column <= W - 2, pltpu.roll(t, cells - 1, 0), 0.0).astype(jnp.bfloat16))


def kernel(
    sizes, act_ref, w_hbm, grad_ref, out_ref, ig_ref, acc,
    actg, gradg, wide, gwide, w, wf, facc, bacc, fpart, bpart, frecv, brecv,
    w_sem, wf_sem, az_send, ay_send, ax_send, gz_send, gy_send, gc_send,
    a_recv, g_recv, f_send, f_recv, b_send, b_recv,
):
    S, NX, NZ, NY = sizes
    cb, cells = act_ref.shape[1:]
    filters, half = grad_ref.shape[1:]
    chans = NX * cb
    s = lax.axis_index("space")
    c = lax.axis_index("chan")
    x = lax.axis_index("filt")
    z, y = s // NY, s % NY
    oy = 1 - y
    f32, bf16 = jnp.float32, jnp.bfloat16

    def remote(src, dst, send, recv, device):
        return pltpu.make_async_remote_copy(
            src_ref=src, dst_ref=dst, send_sem=send, recv_sem=recv,
            device_id=device, device_id_type=MESH,
        )

    def signal(device):
        pl.semaphore_signal(barrier, inc=1, device_id=device, device_id_type=MESH)

    def a_slot(plane, part):
        return actg.at[plane, pl.ds(pl.multiple_of(part * cb, cb), cb), :]

    def g_slot(plane, part):
        return gradg.at[plane + 1, :, pl.ds(pl.multiple_of(part * half, half), half)]

    ypeer = {"space": z * NY + oy}
    xpeers = [{"filt": (x + e) % NX} for e in range(1, NX)]
    cpeer = {"chan": 1 - c}

    def a_copy(plane, send, device):
        slot = a_slot(plane, x)
        return remote(slot, slot, send, a_recv.at[plane * NX + x], device)

    def g_copy(plane, send, device):
        slot = g_slot(plane, c)
        return remote(slot, slot, send, g_recv.at[plane * 2 + c], device)

    def a_wait(plane, part):
        slot = a_slot(plane, part)
        remote(slot, slot, ay_send.at[0], a_recv.at[plane * NX + part], ypeer).wait_recv()

    def g_wait(plane, part):
        slot = g_slot(plane, part)
        remote(slot, slot, gy_send.at[0], g_recv.at[plane * 2 + part], ypeer).wait_recv()

    def a_z(zz, way):
        to = {"space": (z + way) * NY + y}
        return a_copy(zz * NY + y, az_send.at[(way + 1) // 2 * NZ + zz], to)

    def g_z(zz, way):
        to = {"space": (z + way) * NY + y}
        return g_copy(zz * NY + y, gz_send.at[(way + 1) // 2 * NZ + zz], to)

    def a_y(zz):
        return a_copy(zz * NY + y, ay_send.at[zz], ypeer)

    def g_y(zz):
        return g_copy(zz * NY + y, gy_send.at[zz], ypeer)

    def a_x(plane, e):
        return a_copy(plane, ax_send.at[plane * (NX - 1) + e - 1], xpeers[e - 1])

    def g_c(plane):
        return g_copy(plane, gc_send.at[plane], cpeer)

    def start_x(plane):
        for e in range(1, NX):
            a_x(plane, e).start()

    def inside(zz):
        return (zz >= 0) & (zz < NZ)

    def at_distance(d, run):
        @pl.when(inside(z - d))
        def _():
            run(z - d, -1)

        @pl.when((d > 0) & inside(z + d))
        def _():
            run(z + d, 1)

    actg[s, pl.ds(pl.multiple_of(x * cb, cb), cb), :] = act_ref[0]
    gradg[s + 1, :, pl.ds(pl.multiple_of(c * half, half), half)] = grad_ref[0]
    barrier = pltpu.get_barrier_semaphore()
    for way in (-1, 1):
        @pl.when(inside(z + way))
        def _():
            signal({"space": (z + way) * NY + y})
    for peer in [ypeer, cpeer] + xpeers:
        signal(peer)
    beside = (z + NZ - 1) // NZ + (2 * NZ - 2 - z) // NZ
    pl.semaphore_wait(barrier, NX + 1 + beside)

    for way in (-1, 1):
        @pl.when(inside(z + way))
        def _():
            a_z(z, way).start()
    a_y(z).start()
    start_x(s)
    for way in (-1, 1):
        @pl.when(inside(z + way))
        def _():
            g_z(z, way).start()
    g_y(z).start()
    g_c(s).start()
    w_copy = pltpu.make_async_copy(w_hbm, w, w_sem)
    w_copy.start()

    def wf_copy(i):
        a, b, k = i // 9, i // 3 % 3, i % 3
        return pltpu.make_async_copy(
            w_hbm.at[a, b, k], wf.at[a, b, :, k * chans : (k + 1) * chans], wf_sem.at[i]
        )

    for i in range(27):
        wf_copy(i).start()

    for end in (0, S + 1):
        gradg[end] = jnp.zeros((filters, cells), bf16)
        wide[end] = jnp.zeros(wide.shape[1:], bf16)

    @pl.loop(1, S + 1)
    def _(j):
        wide[j, 0:W, :] = jnp.zeros((W, 3 * chans), bf16)
        wide[j, W + cells : 2 * W + cells, :] = jnp.zeros((W, 3 * chans), bf16)

    for j in range(3):
        gwide[j, 0:W, :] = jnp.zeros((W, gwide.shape[2]), bf16)
        gwide[j, W + cells : 2 * W + cells, :] = jnp.zeros((W, gwide.shape[2]), bf16)

    @pl.loop(0, 27)
    def _(i):
        acc[i // 9, i // 3 % 3, i % 3] = jnp.zeros((filters, chans), f32)

    facc[...] = jnp.zeros_like(facc)
    bacc[...] = jnp.zeros_like(bacc)
    w_copy.wait()
    for i in range(27):
        wf_copy(i).wait()

    lanes = gwide.shape[2] // 3

    def b_copy(e):
        to = (x + e) % NX
        return remote(
            bpart.at[pl.ds(pl.multiple_of(to * cb, cb), cb), :],
            brecv.at[e - 1], b_send.at[e - 1], b_recv.at[e - 1], xpeers[e - 1],
        )

    f_copy = remote(
        fpart.at[:, pl.ds(pl.multiple_of((1 - c) * half, half), half)], frecv, f_send, f_recv, cpeer
    )

    def window(plane, b):
        return wide[plane + 1, pl.ds(pl.multiple_of(b * W, W), cells), :]

    def backward():
        @pl.loop(0, 3)
        def _(j):
            def store(k, value):
                at = (2 - k) * lanes
                gwide[j, W : W + cells, at : at + filters] = value

            shifted_copies(gradg[s + j].astype(f32).T, store)

        @pl.loop(0, 3)
        def _(a):
            total = None
            for b in range(3):
                rows = slice((2 - b) * W, (2 - b) * W + cells)
                if lanes == filters:
                    taps = w[a, b].reshape(3 * filters, chans)
                    terms = [jnp.dot(gwide[2 - a, rows, :], taps, preferred_element_type=f32)]
                else:
                    terms = [
                        jnp.dot(
                            gwide[2 - a, rows, k * lanes : k * lanes + filters],
                            w[a, b, k], preferred_element_type=f32,
                        )
                        for k in range(3)
                    ]
                for term in terms:
                    total = term if total is None else total + term
            bacc[...] += total

        bpart[...] = bacc[...].T

    def send_backward():
        for e in range(1, NX):
            b_copy(e).start()

    def forward():
        @pl.loop(0, 3)
        def _(a):
            total = None
            for b in range(3):
                term = lax.dot_general(
                    window(s + a - 1, b), wf[a, b], (((1,), (1,)), ((), ())), preferred_element_type=f32
                )
                total = term if total is None else total + term
            facc[...] += total

        fpart[...] = facc[...].T
        f_copy.start()

    def prepare(zz):
        @pl.loop(0, NY)
        def _(i):
            plane = zz * NY + i
            for e in range(1, NX):
                a_wait(plane, (x + e) % NX)

            def store(k, value):
                wide[plane + 1, W : W + cells, k * chans : (k + 1) * chans] = value

            shifted_copies(actg[plane].astype(f32).T, store)

    scale = 1.0 / math.sqrt(S * cells)

    def add(a, b, value):
        for k in range(3):
            acc[a, b, k] += value[:, k * chans : (k + 1) * chans] * scale

    def in_pair(zz):
        @pl.loop(0, 3)
        def _(b):
            j = zz * NY
            grads = gradg[pl.ds(j + 1, 2)].reshape(2 * filters, cells)
            low = jnp.dot(grads, window(j, b), preferred_element_type=f32)
            high = jnp.dot(grads, window(j + 1, b), preferred_element_type=f32)
            add(0, b, low[filters:])
            add(1, b, low[:filters] + high[filters:])
            add(2, b, high[:filters])

    def across_pairs(zz):
        @pl.loop(0, 3)
        def _(b):
            j = zz * NY + 1
            add(0, b, jnp.dot(gradg[j + 2], window(j, b), preferred_element_type=f32))
            add(2, b, jnp.dot(gradg[j + 1], window(j + 1, b), preferred_element_type=f32))

    def filter_grad(zz, way):
        prepare(zz)
        in_pair(zz)

        @pl.when(zz != z)
        def _():
            across_pairs(zz + (-1 - way) // 2)

    def relay(zz, way, wait, along, across, last):
        plane = zz * NY + y
        wait(plane)

        @pl.when(inside(z - way))
        def _():
            along(zz, -way).start()

        across(zz).start()
        last(plane)

    def pass_on(zz, wait, last):
        plane = zz * NY + oy
        wait(plane)
        last(plane)

    def a_own(plane):
        a_wait(plane, x)

    def g_own(plane):
        g_wait(plane, c)

    def start_c(plane):
        g_c(plane).start()

    def core_halves(zz, way):
        for n in range(NY):
            g_wait(zz * NY + n, 1 - c)

    @pl.loop(1, NZ + 2)
    def _(d):
        at_distance(d - 1, lambda zz, way: pass_on(zz, a_own, start_x))
        at_distance(d, lambda zz, way: relay(zz, way, a_own, a_z, a_y, start_x))
        at_distance(d - 1, lambda zz, way: pass_on(zz, g_own, start_c))
        at_distance(d, lambda zz, way: relay(zz, way, g_own, g_z, g_y, start_c))
        at_distance(d - 1, core_halves)

        @pl.when(d == 2)
        def _():
            backward()

        @pl.when(d == 4)
        def _():
            send_backward()
            forward()

        @pl.when(d != 2)
        def _():
            at_distance(jnp.maximum(d - 2, 0), filter_grad)

    f_copy.wait()
    out_ref[0] = (fpart[:, pl.ds(pl.multiple_of(c * half, half), half)] + frecv[...]).astype(bf16)
    own = bpart[pl.ds(pl.multiple_of(x * cb, cb), cb), :]
    for e in range(1, NX):
        b_copy(e).wait()
        own = own + brecv[e - 1]
    ig_ref[0] = own.astype(bf16)

    @pl.loop(0, NZ)
    def _(zz):
        for way in (-1, 1):
            @pl.when(inside(z + way) & ((z - zz) * way >= 0))
            def _():
                a_z(zz, way).wait_send()
                g_z(zz, way).wait_send()
        a_y(zz).wait_send()
        g_y(zz).wait_send()

    @pl.loop(0, S)
    def _(plane):
        for e in range(1, NX):
            a_x(plane, e).wait_send()
        g_c(plane).wait_send()


def body(activation, weights, out_grad):
    S = lax.axis_size("space")
    NX = lax.axis_size("filt")
    NY = 2
    NZ = S // NY
    cb, cells = activation.shape[1:]
    filters, half = out_grad.shape[1:]
    chans = NX * cb
    bf16, f32 = jnp.bfloat16, jnp.float32
    dma = pltpu.SemaphoreType.DMA
    vmem = pl.BlockSpec(memory_space=pltpu.VMEM)
    hbm = pl.BlockSpec(memory_space=pl.ANY)
    shapes = ((out_grad.shape, bf16), (activation.shape, bf16), (weights.shape, f32))
    results = pl.pallas_call(
        functools.partial(kernel, (S, NX, NZ, NY)),
        out_shape=tuple(pltpu.VMEM(*shape) for shape in shapes),
        in_specs=[vmem, hbm, vmem],
        out_specs=(vmem, vmem, vmem),
        scratch_shapes=[
            pltpu.VMEM((S, chans, cells), bf16),
            pltpu.VMEM((S + 2, filters, cells), bf16),
            pltpu.VMEM((S + 2, cells + 2 * W, 3 * chans), bf16),
            pltpu.VMEM((3, cells + 2 * W, 3 * pl.cdiv(filters, 128) * 128), bf16),
            pltpu.VMEM(weights.shape, bf16),
            pltpu.VMEM((3, 3, filters, 3 * chans), bf16),
            pltpu.VMEM((cells, filters), f32),
            pltpu.VMEM((cells, chans), f32),
            pltpu.VMEM((filters, cells), f32),
            pltpu.VMEM((chans, cells), f32),
            pltpu.VMEM((filters, half), f32),
            pltpu.VMEM((NX - 1, cb, cells), f32),
            dma, dma((27,)),
            dma((2 * NZ,)), dma((NZ,)), dma((S * (NX - 1),)),
            dma((2 * NZ,)), dma((NZ,)), dma((S,)),
            dma((S * NX,)), dma((S * 2,)),
            dma, dma, dma((NX - 1,)), dma((NX - 1,)),
        ],
        compiler_params=pltpu.CompilerParams(
            collective_id=0, has_side_effects=True, vmem_limit_bytes=50 * 1024 * 1024
        ),
    )(activation, weights, out_grad)
    return results


def pair_at(z, y, NZ, o):
    side = 2 * y - 1
    out = jnp.where(z == 0, o, NZ - 1 - o)
    last = jnp.where(z == 1, NZ - 1, 0)
    mid = jnp.where(o == 1, z + side, jnp.where(o == 2, z - side, jnp.where(o == 3, last, z)))
    return jnp.where((z == 0) | (z == NZ - 1), out, mid)


def last_kernel(
    out_ref, ig_ref, acc, gradg, wide, out_hbm, ig_hbm, kg_hbm, stage, out_sem, ig_sem, kg_sem
):
    NY, NZ = 2, 4
    S, filters, cells = gradg.shape
    chans = acc.shape[-1]
    s = lax.axis_index("space")
    z, y = s // NY, s % NY
    oy = 1 - y
    f32 = jnp.float32
    out_copy = pltpu.make_async_copy(out_ref, out_hbm, out_sem)
    ig_copy = pltpu.make_async_copy(ig_ref, ig_hbm, ig_sem)
    out_copy.start()
    ig_copy.start()
    for b in range(1):
        for a in range(3):
            pltpu.make_async_copy(acc.at[a, b], kg_hbm.at[a, b], kg_sem).start()
    zz = pair_at(z, y, NZ, NZ - 1)
    low = jnp.where(zz > z, zz * NY - 1, zz * NY + NY - 1)
    scale = 1.0 / math.sqrt(S * cells)

    def part(value, k):
        return value[:, k * chans : (k + 1) * chans] * scale

    for b in range(1, 3):
        def window(plane):
            return wide[plane, b * W : b * W + cells, :]

        before = jnp.dot(gradg[low + 1], window(low), preferred_element_type=f32)
        after = jnp.dot(gradg[low], window(low + 1), preferred_element_type=f32)
        for k in range(3):
            stage[0, b, k] = acc[0, b, k] + part(before, k)
            stage[1, b, k] = acc[1, b, k]
            stage[2, b, k] = acc[2, b, k] + part(after, k)
        grads = gradg[pl.ds(zz * NY, NY)].reshape(NY * filters, cells)
        value = jnp.dot(grads, window(zz * NY + oy), preferred_element_type=f32)
        for k in range(3):
            stage[oy + 1, b, k] += part(value[:filters], k)
            stage[oy, b, k] += part(value[filters:], k)
        for a in range(3):
            pltpu.make_async_copy(stage.at[a, b], kg_hbm.at[a, b], kg_sem).start()
    out_copy.wait()
    ig_copy.wait()
    pltpu.make_async_copy(stage, kg_hbm, kg_sem).wait()


def near_kernel(
    act_hbm, w_hbm, grad_hbm, out_ref, ig_ref, acc, gradg, wide,
    actg, gwide, w, wf, facc, bacc, fpart, bpart, frecv, brecv,
    in_sem, w_sem, az_send, ay_send, ax_send, gz_send, gy_send, gc_send,
    a_recv, g_recv, f_send, f_recv, b_send, b_recv, p_send,
):
    NY, NZ, H, parts = 2, 4, 1, 2
    S = NY * NZ
    cb, cells = act_hbm.shape[1:]
    filters, half = grad_hbm.shape[1:]
    chans = 2 * cb
    a_rows, g_rows = cb // H, filters // H
    s = lax.axis_index("space")
    c = lax.axis_index("chan")
    x = lax.axis_index("filt")
    z, y = s // NY, s % NY
    oy = 1 - y
    end = (z == 0) | (z == NZ - 1)
    inner = jnp.where(z < NZ // 2, 1, -1)
    f32, bf16 = jnp.float32, jnp.bfloat16
    ypeer = {"space": z * NY + oy}
    xpeer = {"filt": 1 - x}
    cpeer = {"chan": 1 - c}

    def zpeer(way):
        return {"space": (z + way) * NY + y}

    def inside(zz):
        return (zz >= 0) & (zz < NZ)

    def remote(src, dst, send, recv, device):
        return pltpu.make_async_remote_copy(
            src_ref=src, dst_ref=dst, send_sem=send, recv_sem=recv,
            device_id=device, device_id_type=MESH,
        )

    def a_slot(plane, part, h):
        return actg.at[plane, pl.ds(pl.multiple_of(part * cb + h * a_rows, a_rows), a_rows), :]

    def g_slot(plane, part, h):
        return gradg.at[plane, pl.ds(h * g_rows, g_rows), pl.ds(pl.multiple_of(part * half, half), half)]

    def a_copy(plane, h, send, device):
        slot = a_slot(plane, x, h)
        return remote(slot, slot, send, a_recv.at[plane * 2 + x, h], device)

    def g_copy(plane, h, send, device):
        slot = g_slot(plane, c, h)
        return remote(slot, slot, send, g_recv.at[plane * 2 + c, h], device)

    def a_z(zz, way, h):
        return a_copy(zz * NY + y, h, az_send, zpeer(way))

    def g_z(zz, way, h):
        return g_copy(zz * NY + y, h, gz_send, zpeer(way))

    def a_y(zz, h):
        return a_copy(zz * NY + y, h, ay_send, ypeer)

    def g_y(zz, h):
        return g_copy(zz * NY + y, h, gy_send, ypeer)

    def a_x(plane, h):
        return a_copy(plane, h, ax_send, xpeer)

    by_z = jnp.where(end, z + 2 * inner, z - inner)
    pass_on = jnp.where(end, z, z + inner)

    def start_x(plane, h):
        @pl.when((plane != by_z * NY + y) & jnp.logical_not(end & (plane == by_z * NY + oy)))
        def _():
            a_x(plane, h).start()

    def p_copy(plane, h):
        slot = a_slot(plane, 1 - x, h)
        return remote(
            slot, slot, p_send.at[jnp.where(plane % NY == y, 0, 1), h], a_recv.at[plane * 2 + 1 - x, h],
            zpeer(jnp.where(end, inner, -inner)),
        )

    def g_c(plane, h):
        return g_copy(plane, h, gc_send, cpeer)

    def a_wait(plane, part, h):
        slot = a_slot(plane, part, h)
        remote(slot, slot, ax_send, a_recv.at[plane * 2 + part, h], xpeer).wait_recv()

    def g_wait(plane, part, h):
        slot = g_slot(plane, part, h)
        remote(slot, slot, gc_send, g_recv.at[plane * 2 + part, h], cpeer).wait_recv()

    own_a = pltpu.make_async_copy(
        act_hbm.at[0], actg.at[s, pl.ds(pl.multiple_of(x * cb, cb), cb), :], in_sem.at[0]
    )
    own_g = pltpu.make_async_copy(
        grad_hbm.at[0], gradg.at[s, :, pl.ds(pl.multiple_of(c * half, half), half)], in_sem.at[1]
    )
    own_a.start()
    own_g.start()
    barrier = pltpu.get_barrier_semaphore()

    def signal(device):
        pl.semaphore_signal(barrier, inc=1, device_id=device, device_id_type=MESH)

    for way in (-1, 1):
        @pl.when(inside(z + way))
        def _():
            signal(zpeer(way))
    for peer in (ypeer, cpeer, xpeer):
        signal(peer)
    w_copy = pltpu.make_async_copy(w_hbm, w, w_sem.at[0])
    w_copy.start()

    def wf_copy(i):
        a, b, k = i // 9, i // 3 % 3, i % 3
        return pltpu.make_async_copy(
            w_hbm.at[a, b, k], wf.at[a, b, :, k * chans : (k + 1) * chans], w_sem.at[1]
        )

    for i in range(27):
        wf_copy(i).start()

    own_a.wait()
    own_g.wait()
    pl.semaphore_wait(barrier, 3 + (z + NZ - 1) // NZ + (2 * NZ - 2 - z) // NZ)

    for h in range(H):
        for way in (-1, 1):
            @pl.when(inside(z + way))
            def _():
                a_z(z, way, h).start()
        a_y(z, h).start()
        a_x(s, h).start()
        for way in (-1, 1):
            @pl.when(inside(z + way))
            def _():
                g_z(z, way, h).start()
        g_y(z, h).start()
        g_c(s, h).start()

    @pl.loop(0, S)
    def _(j):
        wide[j, 0:W, :] = jnp.zeros((W, 3 * chans), bf16)
        wide[j, W + cells : 2 * W + cells, :] = jnp.zeros((W, 3 * chans), bf16)

    for j in range(3):
        gwide[j, 0:W, :] = jnp.zeros((W, 3 * filters), bf16)
        gwide[j, W + cells : 2 * W + cells, :] = jnp.zeros((W, 3 * filters), bf16)

    @pl.loop(0, 27)
    def _(i):
        acc[i // 9, i // 3 % 3, i % 3] = jnp.zeros((filters, chans), f32)

    def from_z(d, wait, part, along):
        for way in (-1, 1):
            zz = z + way * d

            @pl.when(inside(zz))
            def _():
                for h in range(H):
                    wait(zz * NY + y, part, h)

                    @pl.when(inside(z - way))
                    def _():
                        along(zz, -way, h).start()

    def a_hand(zz):
        @pl.when(inside(zz))
        def _():
            for h in range(H):
                a_y(zz, h).start()
                start_x(zz * NY + y, h)

    def g_hand(zz):
        @pl.when(inside(zz))
        def _():
            for h in range(H):
                g_y(zz, h).start()
                g_c(zz * NY + y, h).start()

    def a_from_z(d):
        from_z(d, a_wait, x, a_z)

    def g_from_z(d):
        from_z(d, g_wait, c, g_z)

    def at_two(hand):
        hand(z + 2)
        hand(z - 2)

    def at_three(hand):
        hand(z + 3)
        hand(z - 3)

    def a_from_y(zz):
        for h in range(H):
            a_wait(zz * NY + oy, x, h)
            start_x(zz * NY + oy, h)

    def g_from_y(zz):
        for h in range(H):
            g_wait(zz * NY + oy, c, h)
            g_c(zz * NY + oy, h).start()

    def a_rest(plane):
        for h in range(H):
            a_wait(plane, 1 - x, h)

    def a_rest_on(plane, go):
        for h in range(H):
            a_wait(plane, 1 - x, h)

            @pl.when(go)
            def _():
                p_copy(plane, h).start()

    def g_rest(plane):
        for h in range(H):
            g_wait(plane, 1 - c, h)

    def window(plane, b):
        return wide[plane, b * W : b * W + cells, :]

    def prepare(plane):
        def store(k, value):
            wide[plane, W : W + cells, k * chans : (k + 1) * chans] = value

        shifted_copies(actg[plane].astype(f32).T, store)

    scale = 1.0 / math.sqrt(S * cells)

    def add(a, b, value):
        for k in range(3):
            acc[a, b, k] += value[:, k * chans : (k + 1) * chans] * scale

    def block(wp, gp, taps=range(3)):
        grad = gradg[gp]
        for b in taps:
            add(wp - gp + 1, b, jnp.dot(grad, window(wp, b), preferred_element_type=f32))

    def in_pair(wp, zz, taps=range(3)):
        grads = gradg[pl.ds(zz * NY, NY)].reshape(NY * filters, cells)
        at = wp - zz * NY
        for b in taps:
            value = jnp.dot(grads, window(wp, b), preferred_element_type=f32)
            add(at + 1, b, value[:filters])
            add(at, b, value[filters:])

    def backward(j, plane):
        def store(k, value):
            at = (2 - k) * filters
            gwide[j, W : W + cells, at : at + filters] = value

        shifted_copies(gradg[plane].astype(f32).T, store)
        a = s + 1 - plane
        total = None
        for b in range(3):
            rows = slice((2 - b) * W, (2 - b) * W + cells)
            taps = w[a, b].reshape(3 * filters, chans)
            term = jnp.dot(gwide[j, rows, :], taps, preferred_element_type=f32)
            total = term if total is None else total + term
        bacc[...] = total if j == 0 else bacc[...] + total

    def forward(j, plane):
        a = plane - s + 1
        total = None
        for b in range(3):
            term = lax.dot_general(
                window(plane, b), wf[a, b], (((1,), (1,)), ((), ())), preferred_element_type=f32
            )
            total = term if total is None else total + term
        facc[...] = total if j == 0 else facc[...] + total

    p_rows = cb // parts

    def b_copy(i):
        return remote(
            bpart.at[pl.ds(pl.multiple_of((1 - x) * cb + i * p_rows, p_rows), p_rows), :],
            brecv.at[pl.ds(i * p_rows, p_rows), :], b_send.at[i], b_recv.at[i], xpeer,
        )

    f_copy = remote(
        fpart.at[:, pl.ds(pl.multiple_of((1 - c) * half, half), half)], frecv, f_send, f_recv, cpeer
    )
    side = 2 * y - 1
    third = s + side
    near_z = jnp.where(end, z + inner, z - side)
    far_z = jnp.where(end, -1, z + side)

    def order(o):
        return pair_at(z, y, NZ, o)

    early = jnp.logical_not(end) & (side != inner)
    exists = (third >= 0) & (third < S)

    other = z * NY + oy
    w_copy.wait()
    g_rest(s)
    backward(0, s)
    a_from_y(z)
    a_from_z(1)
    a_hand(near_z)
    a_rest_on(s, end)
    prepare(s)
    g_from_z(1)
    g_hand(near_z)
    a_hand(far_z)
    g_hand(far_z)
    pltpu.make_async_copy(w_hbm, w, w_sem.at[1]).wait()
    forward(0, s)
    g_from_y(z)
    a_rest(other)
    prepare(other)
    a_from_z(2)
    at_two(a_hand)
    g_rest(other)
    backward(1, other)
    block(s, s)
    forward(1, other)
    a_from_y(order(1))
    block(s, other)
    g_from_z(2)
    at_two(g_hand)
    g_from_y(order(1))
    in_pair(other, z)
    pl.when(jnp.logical_not(end))(lambda: a_rest_on(pass_on * NY + y, z >= 0))
    a_from_y(order(2))
    a_from_z(3)
    at_three(a_hand)

    @pl.loop(1, NZ)
    def _(o):
        zz = order(o)
        mine, theirs = zz * NY + y, zz * NY + oy
        pl.when(end | (zz != pass_on))(lambda: a_rest(mine))
        prepare(mine)

        @pl.when(o == 2)
        def _():
            pl.when(exists)(lambda: forward(2, third))
            fpart[...] = facc[...].T
            f_copy.start()

        g_rest(mine)
        g_rest(theirs)
        in_pair(mine, zz)

        @pl.when(o == 1)
        def _():
            pl.when(exists)(lambda: backward(2, third))
            bpart[...] = bacc[...].T


        @pl.when(o == 2)
        def _():
            b_copy(1).start()
            g_from_y(order(3))

        pl.when(jnp.logical_not(early & (o == 2)))(lambda: a_rest(theirs))
        prepare(theirs)

        @pl.when(o == 1)
        def _():
            g_from_z(3)
            at_three(g_hand)
            b_copy(0).start()

        pl.when(o < NZ - 1)(lambda: in_pair(theirs, zz))

        @pl.when(o == 1)
        def _():
            pl.when(early)(lambda: a_rest(pass_on * NY + oy))
            for h in range(H):
                pl.when(jnp.logical_not(end))(lambda: p_copy(pass_on * NY + oy, h).start())

        low = jnp.where(zz > z, zz * NY - 1, zz * NY + NY - 1)
        pl.when(o < NZ - 1)(lambda: block(low, low + 1))

        @pl.when(o == 1)
        def _():
            g_from_y(order(2))

        pl.when(o < NZ - 1)(lambda: block(low + 1, low))

        @pl.when(o == 1)
        def _():
            a_from_y(order(3))


    zz = order(NZ - 1)
    low = jnp.where(zz > z, zz * NY - 1, zz * NY + NY - 1)
    in_pair(zz * NY + oy, zz, range(1))
    block(low, low + 1, range(1))
    block(low + 1, low, range(1))
    f_copy.wait()
    out_ref[0] = (fpart[:, pl.ds(pl.multiple_of(c * half, half), half)] + frecv[...]).astype(bf16)
    for i in range(parts):
        b_copy(i).wait()
    ig_ref[0] = (bpart[pl.ds(pl.multiple_of(x * cb, cb), cb), :] + brecv[...]).astype(bf16)

    def sent(n, a_send, g_send, a_peer, g_peer):
        a_all = actg.at[0:n, 0:cb, :]
        g_all = gradg.at[0:n, :, 0:half]
        remote(a_all, a_all, a_send, a_recv.at[0, 0], a_peer).wait_send()
        remote(g_all, g_all, g_send, g_recv.at[0, 0], g_peer).wait_send()

    sent(NZ, ay_send, gy_send, ypeer, ypeer)
    def x_sent(n):
        x_all = actg.at[0:n, 0:cb, :]
        remote(x_all, x_all, ax_send, a_recv.at[0, 0], xpeer).wait_send()

    pl.when(end)(lambda: x_sent(S - 2))
    pl.when(jnp.logical_not(end))(lambda: x_sent(S - 1))
    c_all = gradg.at[0:S, :, 0:half]
    remote(c_all, c_all, gc_send, g_recv.at[0, 0], cpeer).wait_send()
    for h in range(H):
        p_copy(pass_on * NY + y, h).wait_send()

        @pl.when(jnp.logical_not(end))
        def _():
            p_copy(pass_on * NY + oy, h).wait_send()
    pl.when(end)(lambda: sent(1, az_send, gz_send, ypeer, ypeer))
    pl.when(jnp.logical_not(end))(lambda: sent(NZ + 1, az_send, gz_send, ypeer, ypeer))


def near_body(activation, weights, out_grad):
    S = lax.axis_size("space")
    NY, H, parts = 2, 1, 2
    NZ = S // NY
    cb, cells = activation.shape[1:]
    filters, half = out_grad.shape[1:]
    chans = 2 * cb
    bf16, f32 = jnp.bfloat16, jnp.float32
    dma = pltpu.SemaphoreType.DMA
    vmem = pl.BlockSpec(memory_space=pltpu.VMEM)
    hbm = pl.BlockSpec(memory_space=pltpu.HBM)
    shapes = ((out_grad.shape, bf16), (activation.shape, bf16), (weights.shape, f32))
    kept = (((S, filters, cells), bf16), ((S, cells + 2 * W, 3 * chans), bf16))
    found = pl.pallas_call(
        near_kernel,
        out_shape=tuple(pltpu.VMEM(*shape) for shape in shapes + kept),
        in_specs=[hbm, hbm, hbm],
        out_specs=(vmem,) * 5,
        scratch_shapes=[
            pltpu.VMEM((S, chans, cells), bf16),
            pltpu.VMEM((3, cells + 2 * W, 3 * filters), bf16),
            pltpu.VMEM(weights.shape, bf16),
            pltpu.VMEM((3, 3, filters, 3 * chans), bf16),
            pltpu.VMEM((cells, filters), f32),
            pltpu.VMEM((cells, chans), f32),
            pltpu.VMEM((filters, cells), f32),
            pltpu.VMEM((chans, cells), f32),
            pltpu.VMEM((filters, half), f32),
            pltpu.VMEM((cb, cells), f32),
            dma((2,)), dma((2,)),
            dma, dma, dma, dma, dma, dma,
            dma((S * 2, H)), dma((S * 2, H)),
            dma, dma, dma((parts,)), dma((parts,)), dma((2, H)),
        ],
        compiler_params=pltpu.CompilerParams(
            collective_id=1, has_side_effects=True, vmem_limit_bytes=45 * 1024 * 1024
        ),
    )(activation, weights, out_grad)
    return pl.pallas_call(
        last_kernel,
        out_shape=tuple(jax.ShapeDtypeStruct(*shape) for shape in shapes),
        in_specs=[vmem] * 5,
        out_specs=(hbm, hbm, hbm),
        scratch_shapes=[pltpu.VMEM(weights.shape, f32), dma, dma, dma],
        compiler_params=pltpu.CompilerParams(vmem_limit_bytes=16 * 1024 * 1024),
    )(*found)


def solution(mesh):
    placed = (
        P("space", ("chan", "filt"), None),
        P(None, None, None, "filt", "chan"),
        P("space", "filt", "chan"),
    )
    near = mesh.shape["space"] == 8 and mesh.shape["filt"] == 2 and mesh.shape["chan"] == 2
    return jax.shard_map(
        near_body if near else body,
        mesh=mesh,
        in_specs=placed,
        out_specs=(
            P("space", "filt", "chan"),
            P("space", ("chan", "filt"), None),
            P(None, None, None, "filt", "chan"),
        ),
        check_vma=False,
    )
```
